32 devices in a mesh: role: 2 (over x), dp: 4 (over z), mp: 4 (over y, core).
Axes of the slice: x: 2, y: 2, z: 4, core: 2. Of those that a mesh axis runs over, the one named last changes fastest.
Arguments:
- state: float32 [2, 2, 8, 256, 512], P('role', None, None, 'dp', 'mp'), may hold values from 0 to 1
- embed: bfloat16 [2, 1024, 4096], P('role', 'dp', 'mp'), may hold values from -0.09375 to 0.09375
- mlp: bfloat16 [2, 2, 1024, 4096], P('role', None, 'dp', 'mp'), may hold values from -0.1875 to 0.1875
- mom_embed: float32 [2, 1024, 4096], P('role', 'dp', 'mp'), may hold values from -6 to 6
- mom_mlp: float32 [2, 2, 1024, 4096], P('role', None, 'dp', 'mp'), may hold values from -6 to 6
Outputs:
- state_out: float32 [2, 8, 256, 512], P(None, None, 'dp', 'mp')
- embed_out: bfloat16 [2, 1024, 4096], P('role', 'dp', 'mp')
- mlp_out: bfloat16 [2, 2, 1024, 4096], P('role', None, 'dp', 'mp')
- mom_embed_out: float32 [2, 1024, 4096], P('role', 'dp', 'mp')
- mom_mlp_out: float32 [2, 2, 1024, 4096], P('role', None, 'dp', 'mp')
The draws below stay inside these ranges and needn't reach their ends.
All inputs are finite; a program needn't handle non-finite values.
Results may differ from the reference program's by a relative error of at most 0.0034.
Values may be sent and summed in bfloat16 or wider, within the bound.
No kernel may reach another device: no remote copies, remote signals or barrier semaphores. Data moves between devices by JAX's collectives and lax.ppermute only.
A program may use at most 128 MiB of HBM per device.

```python
import jax
import jax.numpy as jnp
from jax import lax

PLANES = 8
PATCH = 16
STEPS = 4
D = 1024
FF = 4096
P_SIZE = 4096
NY = 256
NZ = 512
ROWS = 128
NPATCH = 512
N_ROLE = 2
N_DP = 4


def level_of(own_key, shape, split, smallest, top_value):
    gain = 1.0
    for dim, blocks in split:
        heights = jax.random.uniform(jax.random.fold_in(jax.random.fold_in(own_key, 6), dim), (blocks,), jnp.float32, smallest / len(split), top_value / len(split))
        gain = gain * jnp.repeat(jnp.exp(heights), shape[dim] // blocks).reshape((-1,) + (1,) * (len(shape) - 1 - dim))
    return gain


def normal_values(key, dims, scale, most, cuts=(), dtype=jnp.bfloat16):
    array = scale * jax.random.normal(key, dims, jnp.float32)
    if cuts:
        array = array * level_of(key, dims, cuts, -0.22, 0.18)
    return jnp.clip(array, -most, most).astype(dtype)


def setup_inputs(seed: int = 0) -> dict:
    key_list = jax.random.split(jax.random.key(seed), 6)
    state = jnp.clip(1.0 * jax.random.uniform(key_list[0], (N_ROLE, 2, PLANES, NY, NZ), jnp.float32) ** level_of(key_list[0], (N_ROLE, 2, PLANES, NY, NZ), ((0, 2), (3, 4), (4, 4)), -0.2, 0.2), 0.0, 1.0)
    embed = normal_values(key_list[1], (N_ROLE, D, P_SIZE), P_SIZE ** -0.5, 0.09375, ((0, 2), (1, 4), (2, 4)))
    mlp = normal_values(key_list[2], (N_ROLE, 2, D, FF), D ** -0.5, 0.1875, ((0, 2), (2, 4), (3, 4)))
    mom_embed = normal_values(key_list[3], (N_ROLE, D, P_SIZE), 1.0, 6.0, ((0, 2), (1, 4), (2, 4)), jnp.float32)
    mom_mlp = normal_values(key_list[4], (N_ROLE, 2, D, FF), 1.0, 6.0, ((0, 2), (2, 4), (3, 4)), jnp.float32)
    return dict(state=state, embed=embed, mlp=mlp, mom_embed=mom_embed, mom_mlp=mom_mlp)


SUBSTRATE_DIFFUSION = 0.2
CATALYST_DIFFUSION = 0.1
FEED_RATE = 0.037
KILL_RATE = 0.06
TIME_STEP = 0.8
GELU_FACTOR = 0.7978845608028654
MOMENTUM_DECAY = 0.9
LEARNING_RATE = 0.003

def react(padded):
    center = padded[:, :, 1:-1, 1:-1]
    below_plane = jnp.concatenate([center[:, :1], center[:, :-1]], axis=1)
    above_plane = jnp.concatenate([center[:, 1:], center[:, -1:]], axis=1)
    beside = below_plane + above_plane + padded[:, :, :-2, 1:-1] + padded[:, :, 2:, 1:-1]
    beside = beside + padded[:, :, 1:-1, :-2] + padded[:, :, 1:-1, 2:]
    laplace = beside - 6.0 * center
    substrate = center[0]
    catalyst = center[1]
    growth = substrate * catalyst * catalyst
    new_substrate = substrate + TIME_STEP * (SUBSTRATE_DIFFUSION * laplace[0] - growth + FEED_RATE * (1.0 - substrate))
    new_catalyst = catalyst + TIME_STEP * (CATALYST_DIFFUSION * laplace[1] + growth - (FEED_RATE + KILL_RATE) * catalyst)
    return jnp.stack([new_substrate, new_catalyst])

def gelu_slope(preact):
    cubic = 0.044715 * preact * preact * preact
    tangent = jnp.tanh(GELU_FACTOR * (preact + cubic))
    return 0.5 * (1.0 + tangent) + 0.5 * preact * (1.0 - tangent * tangent) * GELU_FACTOR * (1.0 + 3.0 * 0.044715 * preact * preact)

def to_patches(brick):
    extent = brick.shape
    blocks = brick.reshape(extent[0], extent[1], extent[2] // PATCH, PATCH, extent[3] // PATCH, PATCH)
    blocks = blocks.transpose(2, 4, 0, 1, 3, 5)
    return blocks.reshape(extent[2] // PATCH * (extent[3] // PATCH), extent[0] * extent[1] * PATCH * PATCH)

def shard_terms(inputs, targets, embed_full, up_full, down_full, loss_scale):
    embedded = jnp.dot(inputs, embed_full.T, preferred_element_type=jnp.float32)
    recip = lax.rsqrt(lax.optimization_barrier(jnp.mean(embedded * embedded, axis=1, keepdims=True)) + 1e-06)
    normed = (embedded * recip).astype(jnp.bfloat16)
    hidden_pre = jnp.dot(normed, up_full, preferred_element_type=jnp.float32)
    active = jax.nn.gelu(hidden_pre, approximate=True).astype(jnp.bfloat16)
    branch = jnp.dot(active, down_full.T, preferred_element_type=jnp.float32)
    stream = (embedded + branch).astype(jnp.bfloat16)
    predicted = inputs.astype(jnp.float32) + jnp.dot(stream, embed_full, preferred_element_type=jnp.float32)
    residual_grad = ((predicted - targets.astype(jnp.float32)) * loss_scale).astype(jnp.bfloat16)
    stream_grad = jnp.dot(residual_grad, embed_full.T, preferred_element_type=jnp.float32)
    stream_sent = stream_grad.astype(jnp.bfloat16)
    hidden_grad = (jnp.dot(stream_sent, down_full, preferred_element_type=jnp.float32) * gelu_slope(hidden_pre)).astype(jnp.bfloat16)
    normed_grad = jnp.dot(hidden_grad, up_full.T, preferred_element_type=jnp.float32)
    embed_grad = stream_grad + recip * normed_grad - embedded * (recip * recip * recip) * lax.optimization_barrier(jnp.mean(normed_grad * embedded, axis=1, keepdims=True))
    embed_sent = embed_grad.astype(jnp.bfloat16)
    embed_term = jnp.dot(stream.T, residual_grad, preferred_element_type=jnp.float32) + jnp.dot(embed_sent.T, inputs, preferred_element_type=jnp.float32)
    up_term = jnp.dot(normed.T, hidden_grad, preferred_element_type=jnp.float32)
    down_term = jnp.dot(stream_sent.T, active, preferred_element_type=jnp.float32)
    return (embed_term, up_term, down_term)

def reference(state, embed, mlp, mom_embed, mom_mlp):
    cells = state[0]
    for iteration in range(STEPS):
        cells = react(jnp.pad(cells, ((0, 0), (0, 0), (1, 1), (1, 1)), mode='wrap'))
    inputs = to_patches(state[0].astype(jnp.bfloat16)).reshape(N_DP, ROWS, P_SIZE)
    targets = to_patches(cells.astype(jnp.bfloat16)).reshape(N_DP, ROWS, P_SIZE)
    embed_full = embed[1]
    up_full = mlp[1, 0]
    down_full = mlp[1, 1]
    loss_scale = float(NPATCH) ** (-0.5)

    def accumulate(totals, pair):
        terms = shard_terms(pair[0], pair[1], embed_full, up_full, down_full, loss_scale)
        return ((totals[0] + terms[0], totals[1] + terms[1], totals[2] + terms[2]), None)
    start = (jnp.zeros((D, P_SIZE), jnp.float32), jnp.zeros((D, FF), jnp.float32), jnp.zeros((D, FF), jnp.float32))
    grads, unused = lax.scan(accumulate, start, (inputs, targets))
    mom_embed_out = MOMENTUM_DECAY * mom_embed + grads[0][None]
    mom_mlp_out = MOMENTUM_DECAY * mom_mlp + jnp.stack([grads[1], grads[2]])[None]
    embed_out = (embed.astype(jnp.float32) - LEARNING_RATE * mom_embed_out).astype(jnp.bfloat16)
    mlp_out = (mlp.astype(jnp.float32) - LEARNING_RATE * mom_mlp_out).astype(jnp.bfloat16)
    return (cells, embed_out, mlp_out, mom_embed_out, mom_mlp_out)
```

```python
import jax
import jax.numpy as jnp
from jax import lax
from jax.sharding import PartitionSpec as P

PATCH = 16
STEPS = 4


SUBSTRATE_DIFFUSION = 0.2
CATALYST_DIFFUSION = 0.1
FEED_RATE = 0.037
KILL_RATE = 0.06
TIME_STEP = 0.8
GELU_FACTOR = 0.7978845608028654
MOMENTUM_DECAY = 0.9
LEARNING_RATE = 0.003

SOLVER, TRAINER = 0, 1
BF16 = jnp.bfloat16
F32 = jnp.float32


class Digit:
    def __init__(self, axis, stride, size):
        self.axis, self.stride, self.size = axis, stride, size
        self.position = lax.axis_index(axis) // stride % size

    def shifted(self, value, step):
        pairs = []
        for index in range(lax.axis_size(self.axis)):
            digit = index // self.stride % self.size
            pairs.append((index, index + ((digit + step) % self.size - digit) * self.stride))
        return lax.ppermute(value, self.axis, pairs)

    def gathered(self, pick, axis):
        parts = [pick(0)] + [self.shifted(pick(k), k) for k in range(1, self.size)]
        return jnp.concatenate(parts, axis=axis) if self.size > 1 else parts[0]

    def ordered(self, pick):
        parts = [pick(0)] + [self.shifted(pick(k), k) for k in range(1, self.size)]
        slots = []
        for slot in range(self.size):
            value = parts[0]
            for k in range(1, self.size):
                value = jnp.where((self.position - slot) % self.size == k, parts[k], value)
            slots.append(value)
        return jnp.concatenate(slots, axis=0)

    def summed(self, value):
        sent = value.astype(BF16)
        for k in range(1, self.size):
            value = value + self.shifted(sent, k).astype(F32)
        return value


def extended(cells, sides, width):
    for axis, dim in sides:
        count = lax.axis_size(axis)
        head = lax.slice_in_dim(cells, 0, width, axis=dim)
        tail = lax.slice_in_dim(cells, cells.shape[dim] - width, cells.shape[dim], axis=dim)
        cells = jnp.concatenate(
            [
                lax.ppermute(tail, axis, [(i, (i + 1) % count) for i in range(count)]),
                cells,
                lax.ppermute(head, axis, [((i + 1) % count, i) for i in range(count)]),
            ],
            axis=dim,
        )
    return cells


def react(padded):
    center = padded[:, :, 1:-1, 1:-1]
    below_plane = jnp.concatenate([center[:, :1], center[:, :-1]], axis=1)
    above_plane = jnp.concatenate([center[:, 1:], center[:, -1:]], axis=1)
    beside = below_plane + above_plane + padded[:, :, :-2, 1:-1] + padded[:, :, 2:, 1:-1]
    beside = beside + padded[:, :, 1:-1, :-2] + padded[:, :, 1:-1, 2:]
    laplace = beside - 6.0 * center
    substrate = center[0]
    catalyst = center[1]
    growth = substrate * catalyst * catalyst
    new_substrate = substrate + TIME_STEP * (
        SUBSTRATE_DIFFUSION * laplace[0] - growth + FEED_RATE * (1.0 - substrate)
    )
    new_catalyst = catalyst + TIME_STEP * (
        CATALYST_DIFFUSION * laplace[1] + growth - (FEED_RATE + KILL_RATE) * catalyst
    )
    return jnp.stack([new_substrate, new_catalyst])


def advance(cells):
    padded = extended(cells, (("dp", 2), ("mp", 3)), STEPS)
    for iteration in range(STEPS):
        padded = react(padded)
    return padded


def gelu_slope(preact):
    cubic = 0.044715 * preact * preact * preact
    tangent = jnp.tanh(GELU_FACTOR * (preact + cubic))
    return 0.5 * (1.0 + tangent) + 0.5 * preact * (1.0 - tangent * tangent) * GELU_FACTOR * (
        1.0 + 3.0 * 0.044715 * preact * preact
    )


def to_patches(brick):
    extent = brick.shape
    blocks = brick.reshape(
        extent[0], extent[1], extent[2] // PATCH, PATCH, extent[3] // PATCH, PATCH
    )
    blocks = blocks.transpose(2, 4, 0, 1, 3, 5)
    return blocks.reshape(
        extent[2] // PATCH * (extent[3] // PATCH), extent[0] * extent[1] * PATCH * PATCH
    )


def rows_dot(left, right):
    return lax.dot_general(left, right, (((1,), (1,)), ((), ())), preferred_element_type=F32)


def cols_dot(left, right):
    return lax.dot_general(left, right, (((0,), (0,)), ((), ())), preferred_element_type=F32)


def dot(left, right):
    return jnp.dot(left, right, preferred_element_type=F32)


def shards(state, embed, mlp, mom_embed, mom_mlp):
    dp_count, mp_count = lax.axis_size("dp"), lax.axis_size("mp")
    halves = 2 if dp_count % 2 == 0 else 1
    pairs = 2 if mp_count % 2 == 0 else 1
    wide = Digit("dp", dp_count // halves, halves)
    band = Digit("dp", 1, dp_count // halves)
    part = Digit("mp", pairs, mp_count // pairs)
    core = Digit("mp", 1, pairs)
    role = Digit("role", 1, lax.axis_size("role"))
    solving = role.position == SOLVER
    width = embed.shape[1] * dp_count
    own_rows, own_cols = embed.shape[1], embed.shape[2]

    def weights(block):
        held = jnp.where(solving, lax.ppermute(block, "role", [(TRAINER, SOLVER)]), block)
        held = band.gathered(lambda k: held, 0)
        return core.gathered(lambda k: held, 1)

    def spread(patches):
        cut = patches.reshape(patches.shape[0], part.size, core.size, own_cols)

        def features(k):
            target = lax.dynamic_index_in_dim(
                cut, (part.position + k) % part.size, axis=1, keepdims=False
            )
            picked = [
                lax.dynamic_index_in_dim(
                    target, (core.position - t) % core.size, axis=1, keepdims=False
                )
                for t in range(core.size)
            ]
            return jnp.concatenate(picked, axis=1)

        rows = part.ordered(features)
        return wide.ordered(lambda k: rows)

    start_cells = state[0]
    start_patches = to_patches(start_cells.astype(BF16))
    half_rows = start_patches.shape[0] // 2
    arrived_half = lax.ppermute(start_patches[half_rows:], "role", [(SOLVER, TRAINER)])
    inputs = spread(jnp.where(solving, start_patches[:half_rows], arrived_half))

    embed_held = weights(embed[0])
    up_held = weights(mlp[0, 0])
    down_held = weights(mlp[0, 1])

    cells = advance(start_cells)
    arrived = lax.ppermute(cells, "role", [(SOLVER, TRAINER)])
    state_out = jnp.where(solving, cells, arrived)
    end_patches = to_patches(state_out.astype(BF16))
    targets = spread(jnp.where(solving, end_patches[:half_rows], end_patches[half_rows:]))

    def all_rows(feature_like, width_like):
        def to_core(k):
            slot = (-k) % core.size * own_cols
            cuts = [v[:, slot : slot + own_cols] for v in feature_like] + list(width_like)
            return jnp.concatenate(cuts, axis=1) if len(cuts) > 1 else cuts[0]

        both = core.gathered(to_core, 0)

        def to_band(k):
            slot = (-k) % band.size * own_rows
            base = len(feature_like) * own_cols
            cuts = [both[:, :base]] if base else []
            for index in range(len(width_like)):
                first = base + index * own_rows * band.size + slot
                cuts.append(both[:, first : first + own_rows])
            return jnp.concatenate(cuts, axis=1) if len(cuts) > 1 else cuts[0]

        banded = band.gathered(to_band, 0)
        whole = role.gathered(lambda k: banded, 0)
        pieces = []
        first = 0
        for size in [own_cols] * len(feature_like) + [own_rows] * len(width_like):
            pieces.append(whole[:, first : first + size])
            first += size
        return pieces

    total_rows = inputs.shape[0] * core.size * band.size * role.size
    loss_scale = float(total_rows) ** (-0.5)

    embedded = part.summed(rows_dot(inputs, embed_held))
    squares = jnp.sum(embedded * embedded, axis=1, keepdims=True)
    for k in range(1, wide.size):
        squares = squares + wide.shifted(squares, k)
    recip = lax.rsqrt(squares / width + 1e-06)
    hidden_pre = wide.summed(dot(embedded.astype(BF16), up_held)) * recip
    normed = (embedded * recip).astype(BF16)
    active = jax.nn.gelu(hidden_pre, approximate=True).astype(BF16)
    branch = part.summed(rows_dot(active, down_held))
    stream = (embedded + branch).astype(BF16)
    predicted = inputs.astype(F32) + wide.summed(dot(stream, embed_held))
    residual = ((predicted - targets.astype(F32)) * loss_scale).astype(BF16)
    stream_grad = part.summed(rows_dot(residual, embed_held))
    stream_sent = stream_grad.astype(BF16)
    hidden_grad = (wide.summed(dot(stream_sent, down_held)) * gelu_slope(hidden_pre)).astype(BF16)
    normed_grad = part.summed(rows_dot(hidden_grad, up_held))
    inner = jnp.sum(hidden_grad.astype(F32) * hidden_pre, axis=1, keepdims=True)
    for k in range(1, part.size):
        inner = inner + part.shifted(inner, k)
    embed_grad = stream_grad + recip * normed_grad - embedded * (recip * recip) * (inner / width)
    embed_sent = embed_grad.astype(BF16)

    (all_inputs,) = all_rows([inputs], [])
    all_active, all_normed, all_stream = all_rows([active], [normed, stream])
    all_residual, all_stream_sent = all_rows([residual], [stream_sent])
    (all_hidden_grad,) = all_rows([hidden_grad], [])
    (all_embed_sent,) = all_rows([], [embed_sent])

    grad_down = cols_dot(all_stream_sent, all_active)
    grad_up = cols_dot(all_normed, all_hidden_grad)
    grad_embed = cols_dot(all_stream, all_residual) + cols_dot(all_embed_sent, all_inputs)

    mom_embed_out = MOMENTUM_DECAY * mom_embed + grad_embed[None]
    mom_mlp_out = MOMENTUM_DECAY * mom_mlp + jnp.stack([grad_up, grad_down])[None]
    embed_out = (embed.astype(F32) - LEARNING_RATE * mom_embed_out).astype(BF16)
    mlp_out = (mlp.astype(F32) - LEARNING_RATE * mom_mlp_out).astype(BF16)
    return (state_out, embed_out, mlp_out, mom_embed_out, mom_mlp_out)


def solution(mesh):
    placed = (
        P("role", None, None, "dp", "mp"),
        P("role", "dp", "mp"),
        P("role", None, "dp", "mp"),
        P("role", "dp", "mp"),
        P("role", None, "dp", "mp"),
    )
    return jax.shard_map(
        shards,
        mesh=mesh,
        in_specs=placed,
        out_specs=(
            P(None, None, "dp", "mp"),
            P("role", "dp", "mp"),
            P("role", None, "dp", "mp"),
            P("role", "dp", "mp"),
            P("role", None, "dp", "mp"),
        ),
        check_vma=False,
    )
```

```python
import jax
import jax.numpy as jnp
from jax import lax
from jax.experimental import pallas as pl
from jax.experimental.pallas import tpu as pltpu
from jax.sharding import PartitionSpec as P

PATCH = 16
STEPS = 4


SUBSTRATE_DIFFUSION = 0.2
CATALYST_DIFFUSION = 0.1
FEED_RATE = 0.037
KILL_RATE = 0.06
TIME_STEP = 0.8
GELU_FACTOR = 0.7978845608028654
MOMENTUM_DECAY = 0.9
LEARNING_RATE = 0.003

SOLVER, TRAINER = 0, 1
BF16 = jnp.bfloat16
F32 = jnp.float32


class Digit:
    def __init__(self, axis, stride, size):
        self.axis, self.stride, self.size = axis, stride, size

    def shifted(self, value, step):
        pairs = []
        for index in range(lax.axis_size(self.axis)):
            digit = index // self.stride % self.size
            pairs.append((index, index + ((digit + step) % self.size - digit) * self.stride))
        return lax.ppermute(value, self.axis, pairs)

    def from_others(self, value):
        return [self.shifted(value, k) for k in range(1, self.size)]


def rows_dot(left, right):
    return lax.dot_general(left, right, (((1,), (1,)), ((), ())), preferred_element_type=F32)


def cols_dot(left, right):
    return lax.dot_general(left, right, (((0,), (0,)), ((), ())), preferred_element_type=F32)


def dot(left, right):
    return jnp.dot(left, right, preferred_element_type=F32)


def struct(shape, dtype):
    return jax.ShapeDtypeStruct(shape, dtype)


TOKEN = (8, 128)
CHEAP = pl.CostEstimate(flops=1, transcendentals=0, bytes_accessed=1)


class Work:
    def __init__(self, body, outs, args, in_hbm=(), scratch=(), aliases=None, extra=(), left=()):
        self.body, self.outs, self.args = body, list(outs), list(args)
        self.in_hbm, self.scratch, self.aliases = in_hbm, list(scratch), aliases or {}
        self.extra, self.left, self.results = list(extra), left, None


class Order:
    def __init__(self):
        self.token, self.pending, self.riders = None, [], []

    def wait_for(self, arrays):
        self.pending = self.pending + list(arrays)

    def ride(self, *args, **kwargs):
        self.riders.append(Work(*args, **kwargs))
        return self.riders[-1]

    def run(self, name):
        last = self.riders.pop()
        last.results = self.call(
            last.body,
            name,
            last.outs,
            last.args,
            in_hbm=last.in_hbm,
            scratch=last.scratch,
            left=last.left,
        )

    def call(self, body, name, outs, args, **kwargs):
        works = self.riders + [Work(body, outs, args, **kwargs)]
        after = ([] if self.token is None else [self.token]) + self.pending
        self.pending, self.riders = [], []
        vmem, anywhere = pl.BlockSpec(memory_space=pltpu.VMEM), pl.BlockSpec(memory_space=pl.ANY)
        args, in_specs, outs, out_specs, scratch, aliases, room = [], [], [], [], [], {}, 0
        spans = []
        for work in works:
            spans.append((len(args), len(outs), len(scratch)))
            for index, target in work.aliases.items():
                aliases[len(args) + index] = len(outs) + target
            for k, value in enumerate(work.args):
                in_specs.append(anywhere if k in work.left else vmem)
                room += 0 if k in work.left else value.size * value.dtype.itemsize
            for k, value in enumerate(work.outs):
                out_specs.append(anywhere if k in work.in_hbm else vmem)
                room += 0 if k in work.in_hbm else value.size * value.dtype.itemsize
            in_specs += [anywhere] * len(work.extra)
            args += work.args + work.extra
            outs += work.outs
            scratch += work.scratch
        in_count, out_count = len(args) + len(after), len(outs) + 1

        def kernel(*refs):
            ins, outs_refs, scratch_refs = (
                refs[:in_count],
                refs[in_count : in_count + out_count],
                refs[in_count + out_count :],
            )
            outs_refs[-1][...] = jnp.zeros(TOKEN, F32)
            for work, (first, out, extra) in zip(works, spans):
                work.body(
                    ins[first : first + len(work.args)],
                    outs_refs[out : out + len(work.outs)],
                    scratch_refs[extra : extra + len(work.scratch)],
                )

        *results, self.token = pl.pallas_call(
            kernel,
            name=name,
            out_shape=outs + [struct(TOKEN, F32)],
            in_specs=in_specs + [anywhere] * len(after),
            out_specs=out_specs + [vmem],
            scratch_shapes=scratch,
            input_output_aliases=aliases,
            compiler_params=pltpu.CompilerParams(
                vmem_limit_bytes=min(56 * 2**20, room + 12 * 2**20)
            ),
            cost_estimate=CHEAP,
        )(*args, *after)
        for work, (_, out, _) in zip(works, spans):
            work.results = results[out : out + len(work.outs)]
        return works[-1].results


class Matrix:
    def __init__(self, pieces):
        self.pieces = pieces
        self.row_count, self.col_count = len(pieces), len(pieces[0])
        self.flat = [piece for row in pieces for piece in row]
        self.rows = sum(row[0].shape[0] for row in pieces)
        self.cols = sum(piece.shape[1] for piece in pieces[0])

    def grid(self, refs):
        return [
            refs[index * self.col_count : (index + 1) * self.col_count]
            for index in range(self.row_count)
        ]

    def to_width(self, refs, value):
        done = []
        for row in self.grid(refs):
            total, first = None, 0
            for ref in row:
                term = rows_dot(value[:, first : first + ref.shape[1]], ref[...])
                total = term if total is None else total + term
                first += ref.shape[1]
            done.append(total)
        return jnp.concatenate(done, axis=1) if len(done) > 1 else done[0]

    def to_cols(self, refs, value):
        done = []
        for col in range(self.col_count):
            total, first = None, 0
            for row in self.grid(refs):
                ref = row[col]
                term = dot(value[:, first : first + ref.shape[0]], ref[...])
                total = term if total is None else total + term
                first += ref.shape[0]
            done.append(total)
        return jnp.concatenate(done, axis=1) if len(done) > 1 else done[0]


LANES = 128


def with_scalars(value, column):
    high = column.astype(BF16).astype(F32)
    low = column - high
    lane = lax.broadcasted_iota(jnp.int32, (value.shape[0], LANES), 1)
    extra = jnp.where(lane == 0, high, jnp.where(lane == 1, low, 0.0))
    return jnp.concatenate([value.astype(BF16), extra.astype(BF16)], axis=1)


def scalars_of(received):
    extra = received[:, received.shape[1] - LANES :].astype(F32)
    return jnp.sum(extra, axis=1, keepdims=True)


def swapped_tiles(cells):
    count = cells.shape[0]
    row = lax.broadcasted_iota(jnp.int32, cells.shape, 0)
    run = lax.broadcasted_iota(jnp.int32, cells.shape, 1) // PATCH
    for bit in (1, 2, 4):
        row_set, run_set = (row & bit) != 0, (run & bit) != 0
        moved = jnp.where(
            row_set, pltpu.roll(cells, bit, 0), pltpu.roll(cells, count - bit, 0)
        )
        shift = bit * PATCH
        moved = jnp.where(
            run_set, pltpu.roll(moved, shift, 1), pltpu.roll(moved, LANES - shift, 1)
        )
        cells = jnp.where(row_set == run_set, cells, moved)
    return cells


def write_patches(tile, outs):
    bands = len(outs)
    species, planes = tile.counts
    for s in range(species):
        for p in range(planes):
            plane = swapped_tiles(tile(s, p))
            octets = PATCH // 8
            groups = plane.shape[0] // PATCH
            each = groups // bands
            for o in range(octets):
                col = ((s * planes + p) * octets + o) * LANES
                for index, out in enumerate(outs):
                    rows = [
                        plane[(g * octets + o) * 8 : (g * octets + o + 1) * 8]
                        for g in range(index * each, (index + 1) * each)
                    ]
                    out[:, col : col + LANES] = jnp.concatenate(rows, axis=0).astype(BF16)


class Tile:
    def __init__(self, read, counts):
        self.read, self.counts = read, counts

    def __call__(self, s, p):
        return self.read(s, p)


def packed_edges(order, cells, head_rows, tail_rows, width):
    species, planes, rows, _ = cells.shape
    tall = rows + 2 * width

    def body(ins, outs, _):
        middle, head, tail = ins
        lane = lax.broadcasted_iota(jnp.int32, (tall, LANES), 1)
        total = jnp.zeros((tall, LANES), F32)
        for s in range(species):
            for p in range(planes):
                plane = jnp.concatenate([head[s, p], middle[s, p], tail[s, p]], axis=0)
                slot = (s * planes + p) * width
                first = plane if slot == 0 else pltpu.roll(plane, slot, 1)
                last = pltpu.roll(plane, (LANES // 2 + slot + width) % LANES, 1)
                total = jnp.where((lane >= slot) & (lane < slot + width), first, total)
                start = LANES // 2 + slot
                total = jnp.where((lane >= start) & (lane < start + width), last, total)
        outs[0][...] = total

    return order.ride(body, [struct((tall, LANES), F32)], [cells, head_rows, tail_rows])


def stepped(order, cells, head_rows, tail_rows, from_left, from_right, width, halves):
    species, planes, rows, cols = cells.shape
    tall = rows + 2 * width
    patch_rows = rows // PATCH * (cols // PATCH) // halves
    features = species * planes * PATCH * PATCH

    def body(ins, outs, scratch):
        middle, head, tail, left, right = ins
        (final, *patches), (now, later) = outs, scratch
        lane = lax.broadcasted_iota(jnp.int32, (tall, LANES), 1)
        from_l, from_r = left[...], right[...]
        for s in range(species):
            for p in range(planes):
                slot = (s * planes + p) * width
                now[0, s, p] = jnp.concatenate([head[s, p], middle[s, p], tail[s, p]], axis=0)
                ahead = from_r if slot == 0 else pltpu.roll(from_r, LANES - slot, 1)
                behind = pltpu.roll(from_l, LANES // 2 - slot - width, 1)
                halo = jnp.where(lane < width, ahead, 0.0)
                now[1, s, p] = jnp.where(lane >= LANES - width, behind, halo)

        def neighbours(field, halo):
            up_f, down_f = pltpu.roll(field, 1, 0), pltpu.roll(field, tall - 1, 0)
            up_h, down_h = pltpu.roll(halo, 1, 0), pltpu.roll(halo, tall - 1, 0)
            before_f, before_h = pltpu.roll(field, 1, 1), pltpu.roll(halo, 1, 1)
            after_f, after_h = pltpu.roll(field, LANES - 1, 1), pltpu.roll(halo, LANES - 1, 1)
            first, last = lane == 0, lane == LANES - 1
            sum_f = up_f + down_f + jnp.where(first, before_h, before_f)
            sum_f = sum_f + jnp.where(last, after_h, after_f)
            sum_h = up_h + down_h + jnp.where(first, before_f, before_h)
            sum_h = sum_h + jnp.where(last, after_f, after_h)
            return sum_f, sum_h

        for step in range(STEPS):
            source, target = (now, later) if step % 2 == 0 else (later, now)

            def one_plane(p, carry):
                below, above = jnp.maximum(p - 1, 0), jnp.minimum(p + 1, planes - 1)
                beside = [neighbours(source[0, s, p], source[1, s, p]) for s in range(2)]
                for layer in range(2):
                    u, v = source[layer, 0, p], source[layer, 1, p]
                    lap = []
                    for s, centre in ((0, u), (1, v)):
                        total = source[layer, s, below] + source[layer, s, above]
                        lap.append(total + beside[s][layer] - 6.0 * centre)
                    growth = u * v * v
                    target[layer, 0, p] = u + TIME_STEP * (
                        SUBSTRATE_DIFFUSION * lap[0] - growth + FEED_RATE * (1.0 - u)
                    )
                    target[layer, 1, p] = v + TIME_STEP * (
                        CATALYST_DIFFUSION * lap[1] + growth - (FEED_RATE + KILL_RATE) * v
                    )
                return carry

            lax.fori_loop(0, planes, one_plane, 0)
        source = now if STEPS % 2 == 0 else later
        for s in range(species):
            for p in range(planes):
                final[s, p] = source[0, s, p, width : width + rows]
        write_patches(Tile(lambda s, p: final[s, p], (species, planes)), patches)

    return order.call(
        body,
        "stencil",
        [struct(cells.shape, F32)] + [struct((patch_rows, features), BF16)] * halves,
        [cells, head_rows, tail_rows, from_left, from_right],
        scratch=[pltpu.VMEM((2, species, planes, tall, LANES), F32)] * 2,
    )


def gelu_parts(preact):
    squared = preact * preact
    tangent = jnp.tanh(GELU_FACTOR * (preact + 0.044715 * preact * squared))
    return squared, tangent


def shards(state, embed, mlp, mom_embed, mom_mlp):
    dp_count, mp_count = lax.axis_size("dp"), lax.axis_size("mp")
    halves = 2 if dp_count % 2 == 0 else 1
    pairs = 2 if mp_count % 2 == 0 else 1
    wide = Digit("dp", dp_count // halves, halves)
    band = Digit("dp", 1, dp_count // halves)
    part = Digit("mp", pairs, mp_count // pairs)
    core = Digit("mp", 1, pairs)
    role = Digit("role", 1, lax.axis_size("role"))
    width = embed.shape[1] * dp_count
    own_rows, own_cols = embed.shape[1], embed.shape[2]
    half_width, part_cols = own_rows * band.size, own_cols * core.size
    to_solver, to_trainer = [(TRAINER, SOLVER)], [(SOLVER, TRAINER)]
    order = Order()

    def keep_arrived(arrived, own, index, following, next_index):
        def body(ins, outs, scratch):
            (sems,) = scratch
            solving = lax.axis_index("role") == SOLVER
            ahead = pltpu.make_async_copy(ins[2].at[next_index], outs[1], sems.at[0])
            ahead.start()

            @pl.when(solving)
            def _():
                outs[0][...] = ins[0][...]

            @pl.when(jnp.logical_not(solving))
            def _():
                mine = pltpu.make_async_copy(ins[1].at[index], outs[0], sems.at[1])
                mine.start()
                mine.wait()

            ahead.wait()

        sent = following.shape[len(next_index) :]
        outs = [struct(arrived.shape, BF16), struct(sent, following.dtype)]
        return order.call(
            body,
            "held",
            outs,
            [arrived, own, following],
            left=(1, 2),
            scratch=[pltpu.SemaphoreType.DMA((2,))],
        )

    def relayed(blocks):
        def body(ins, outs, _):
            for source, target in zip(ins, outs):
                target[...] = source[...]

        return order.ride(body, [struct(v.shape, v.dtype) for v in blocks], blocks)

    def own_pieces(block):
        return [block] + core.from_others(block), band.from_others(block)

    def merged(parts):
        return [jnp.concatenate(parts, axis=0)] if len(parts) > 1 else parts

    def held_matrix(own, relay):
        return Matrix([own] + [[rows] + core.from_others(rows) for rows in relay.results])

    cells = state[0]
    rows_in = cells.shape[2]
    features = cells.shape[0] * cells.shape[1] * PATCH * PATCH
    half_rows = rows_in // PATCH * (cells.shape[3] // PATCH) // 2

    def around(axis, step):
        count = lax.axis_size(axis)
        return [(i, (i + step) % count) for i in range(count)]

    def patches_of(ins, outs, _):
        counts = (cells.shape[0], cells.shape[1])
        write_patches(Tile(lambda s, p: ins[0][s, p], counts), outs[:2])
        outs[2][...] = ins[0][:, :, :STEPS]
        outs[3][...] = ins[0][:, :, rows_in - STEPS :]

    def split_patches(own, arrived):
        def body(ins, outs, _):
            solving = lax.axis_index("role") == SOLVER
            position = lax.axis_index("mp")
            my_part, my_core = position // core.size, position % core.size
            for k in range(part.size):
                for t in range(core.size):
                    quarter = (my_part + k) % part.size * core.size
                    quarter = quarter + (my_core - t + core.size) % core.size
                    source = pl.ds(pl.multiple_of(quarter * own_cols, own_cols), own_cols)
                    cols = slice(t * own_cols, (t + 1) * own_cols)

                    @pl.when(solving)
                    def _():
                        outs[k][:, cols] = ins[0][:, source]

                    @pl.when(jnp.logical_not(solving))
                    def _():
                        outs[k][:, cols] = ins[1][:, source]

        return order.ride(
            body, [struct((half_rows, part_cols), BF16)] * part.size, [own, arrived]
        )

    def to_parts(cuts):
        return [cuts[0]] + [part.shifted(cuts[k], k) for k in range(1, part.size)]

    def slots(position, size, count):
        for k in range(size):
            slot = (position - k + size) % size
            yield k, pl.ds(pl.multiple_of(slot * count, count), count)

    def order_rows(pieces):
        def body(ins, outs, _):
            for k, rows in slots(lax.axis_index("mp") // core.size, part.size, half_rows):
                outs[0][rows, :] = ins[k][...]

        return order.ride(body, [struct((half_rows * part.size, part_cols), BF16)], pieces)

    def widened(rows):
        return [rows] + wide.from_others(rows)

    def pack(has_features, width_count):
        return struct((m, (own_cols if has_features else 0) + width_count * half_width), BF16)

    class Gather:
        def __init__(self, keep, sends, has_features, width_count):
            self.base = own_cols if has_features else 0
            self.width_count = width_count
            self.parts = [keep] + [core.shifted(sends[k - 1], k) for k in range(1, core.size)]

        def join(self):
            count = band.size if self.width_count else 1
            base = self.base

            def body(ins, outs, _):
                for c, ref in enumerate(ins):
                    rows = slice(c * m, (c + 1) * m)
                    for k in range(count):
                        if base:
                            outs[k][rows, :base] = ref[:, :base]
                        for index in range(self.width_count):
                            first = base + index * half_width + (-k) % band.size * own_rows
                            target = base + index * own_rows
                            outs[k][rows, target : target + own_rows] = ref[
                                :, first : first + own_rows
                            ]

            cols = base + self.width_count * own_rows
            self.joining = order.ride(
                body, [struct((m * core.size, cols), BF16)] * count, self.parts
            )

        def send(self):
            cuts = self.joining.results
            self.kept = cuts[0]
            self.banded = merged(
                [band.shifted(cuts[k % len(cuts)], k) for k in range(1, band.size)]
            )
            self.arrived = role.from_others(self.kept)

        def relay(self):
            self.relaying = relayed(self.banded)

        def forward(self, relayed_too=True):
            self.banded = self.relaying.results if relayed_too else self.banded
            for piece in self.banded:
                self.arrived = self.arrived + role.from_others(piece)

        def pieces(self):
            return [self.kept] + self.banded + self.arrived

    def selected_state(own, arrived):
        def body(ins, outs, scratch):
            solving = lax.axis_index("role") == SOLVER
            (sem,) = scratch
            for chosen, source in ((solving, ins[0]), (jnp.logical_not(solving), ins[1])):

                @pl.when(chosen)
                def _():
                    copy = pltpu.make_async_copy(source, outs[0], sem)
                    copy.start()
                    copy.wait()

        scratch = [pltpu.SemaphoreType.DMA]
        outs = [struct(own.shape, F32)]
        return order.call(body, "state", outs, [own, arrived], in_hbm=(0,), scratch=scratch)[0]

    m = half_rows * part.size * wide.size
    total_rows = m * core.size * band.size * role.size
    loss_scale = float(total_rows) ** (-0.5)

    arrived_embed = lax.ppermute(embed[0], "role", to_solver)
    edge_struct = struct(cells.shape[:2] + (STEPS, cells.shape[3]), F32)
    *start_halves, first_rows, last_rows = order.call(
        patches_of,
        "patches",
        [struct((half_rows, features), BF16)] * 2 + [edge_struct] * 2,
        [cells],
    )
    arrived_start = lax.ppermute(start_halves[1], "role", to_trainer)
    head_rows = lax.ppermute(last_rows, "dp", around("dp", 1))
    tail_rows = lax.ppermute(first_rows, "dp", around("dp", -1))
    splitting = split_patches(start_halves[0], arrived_start)
    order.run("split")
    ordering = order_rows(to_parts(splitting.results))
    edging = packed_edges(order, cells, head_rows, tail_rows, STEPS)
    embed_kept, up_block = keep_arrived(arrived_embed, embed, 0, mlp, (0, 0))
    embed_own, embed_bands = own_pieces(embed_kept)
    arrived_up = lax.ppermute(up_block, "role", to_solver)
    input_parts = widened(*ordering.results)
    (edges,) = edging.results
    from_left = lax.ppermute(edges, "mp", around("mp", 1))
    from_right = lax.ppermute(edges, "mp", around("mp", -1))
    relay = relayed(merged(embed_bands))
    order.wait_for([from_left, from_right] + input_parts[1:])
    up_kept, down_block = keep_arrived(arrived_up, mlp, (0, 0), mlp, (0, 1))
    up_own, up_bands = own_pieces(up_kept)
    arrived_down = lax.ppermute(down_block, "role", to_solver)
    embed_held = held_matrix(embed_own, relay)

    def embed_rows(ins, outs, _):
        parts, matrix = ins[: wide.size], ins[wide.size :]
        *inputs, mine, sent = outs
        position = lax.axis_index("dp") // band.size
        for k, rows in slots(position, wide.size, half_rows * part.size):
            for t in range(core.size):
                inputs[t][rows, :] = parts[k][:, t * own_cols : (t + 1) * own_cols]
        value = embed_held.to_width(matrix, jnp.concatenate([ref[...] for ref in inputs], axis=1))
        mine[...] = value
        sent[...] = value.astype(BF16)

    *inputs, embed_mine, embed_sum = order.call(
        embed_rows,
        "embed",
        [struct((m, own_cols), BF16)] * core.size
        + [struct((m, half_width), F32), struct((m, half_width), BF16)],
        input_parts + embed_held.flat,
    )
    embed_others = part.from_others(embed_sum)

    def core_slot(k):
        return slice((-k) % core.size * own_cols, ((-k) % core.size + 1) * own_cols)

    final_cells, *end_halves = stepped(
        order, cells, head_rows, tail_rows, from_left, from_right, STEPS, 2
    )
    arrived_end = lax.ppermute(end_halves[1], "role", to_trainer)
    relay = relayed(merged(up_bands))
    down_kept, cells_sent = keep_arrived(arrived_down, mlp, (0, 1), final_cells, ())
    down_own, down_bands = own_pieces(down_kept)
    arrived_cells = lax.ppermute(cells_sent, "role", to_trainer)
    up_held = held_matrix(up_own, relay)
    inputs_on = Gather(inputs[0], [inputs[(-k) % core.size] for k in range(1, core.size)], True, 0)

    def added(mine, refs, cols):
        total = mine[...]
        for ref in refs:
            total = total + ref[:, :cols].astype(F32)
        return total

    def up_rows(ins, outs, _):
        others, matrix = ins[1 : part.size], ins[part.size :]
        embedded, mine, sent = outs
        value = added(ins[0], others, half_width)
        embedded[...] = value
        hidden = up_held.to_cols(matrix, value.astype(BF16))
        mine[...] = hidden
        sent[...] = with_scalars(hidden, jnp.sum(value * value, axis=1, keepdims=True))

    embedded, up_mine, up_sum = order.call(
        up_rows,
        "up",
        [
            struct((m, half_width), F32),
            struct((m, part_cols), F32),
            struct((m, part_cols + LANES), BF16),
        ],
        [embed_mine] + embed_others + up_held.flat,
    )
    up_others = wide.from_others(up_sum)
    order.wait_for(up_others + [arrived_cells])
    inputs_on.join()
    splitting = split_patches(end_halves[0], arrived_end)
    relay = relayed(merged(down_bands))
    order.run("relay")
    down_held = held_matrix(down_own, relay)
    inputs_on.send()
    ordering = order_rows(to_parts(splitting.results))

    def down_rows(ins, outs, _):
        value, others, matrix = ins[0][...], ins[2 : 1 + wide.size], ins[1 + wide.size :]
        hidden, mine, sent, scale, *packs = outs
        squares = jnp.sum(value * value, axis=1, keepdims=True)
        for ref in others:
            squares = squares + scalars_of(ref)
        recip = lax.rsqrt(squares / width + 1e-06)
        preact = added(ins[1], others, part_cols) * recip
        hidden[...] = preact
        normed = (value * recip).astype(BF16)
        _, tangent = gelu_parts(preact)
        active = (0.5 * preact * (1.0 + tangent)).astype(BF16)
        branch = down_held.to_width(matrix, active)
        mine[...] = branch
        sent[...] = branch.astype(BF16)
        scale[...] = jnp.broadcast_to(recip, scale.shape)
        for k in range(core.size):
            packs[k][:, :own_cols] = active[:, core_slot(k)]
            packs[k][:, own_cols:] = normed

    hidden_pre, down_mine, down_sum, scale, *active_packs = order.call(
        down_rows,
        "down",
        [
            struct((m, part_cols), F32),
            struct((m, half_width), F32),
            struct((m, half_width), BF16),
            struct((m, LANES), F32),
        ]
        + [pack(True, 1)] * core.size,
        [embedded, up_mine] + up_others + down_held.flat,
    )
    down_others = part.from_others(down_sum)
    target_parts = widened(*ordering.results)
    active_on = Gather(active_packs[0], active_packs[1:], True, 1)
    inputs_on.relay()
    active_on.join()

    def predict_rows(ins, outs, _):
        others, matrix = ins[2 : 1 + part.size], ins[1 + part.size :]
        mine, sent, stream = outs
        value = (ins[0][...] + added(ins[1], others, half_width)).astype(BF16)
        stream[...] = value
        predicted = embed_held.to_cols(matrix, value)
        mine[...] = predicted
        sent[...] = predicted.astype(BF16)

    predict_mine, predict_sum, stream = order.call(
        predict_rows,
        "predict",
        [
            struct((m, part_cols), F32),
            struct((m, part_cols), BF16),
            struct((m, half_width), BF16),
        ],
        [embedded, down_mine] + down_others + embed_held.flat,
    )
    predict_others = wide.from_others(predict_sum)
    inputs_on.forward()
    active_on.send()
    active_on.relay()
    order.wait_for(inputs_on.arrived)

    def residual_rows(ins, outs, scratch):
        inputs, ins = ins[: core.size], ins[core.size :]
        mine_in, others, ins = ins[0], ins[1 : wide.size], ins[wide.size :]
        aims, stream, matrix = ins[: wide.size], ins[wide.size], ins[wide.size + 1 :]
        mine, sent, *packs = outs
        (aim,) = scratch
        position = lax.axis_index("dp") // band.size
        for k, rows in slots(position, wide.size, half_rows * part.size):
            aim[rows, :] = aims[k][...]
        known = jnp.concatenate([ref[...] for ref in inputs], axis=1).astype(F32)
        predicted = known + added(mine_in, others, part_cols)
        value = ((predicted - aim[...].astype(F32)) * loss_scale).astype(BF16)
        for k in range(core.size):
            packs[k][:, :own_cols] = value[:, core_slot(k)]
            packs[k][:, own_cols:] = stream[...]
        grad = embed_held.to_width(matrix, value)
        mine[...] = grad
        sent[...] = grad.astype(BF16)

    stream_mine, stream_sum, *residual_packs = order.call(
        residual_rows,
        "residual",
        [struct((m, half_width), F32), struct((m, half_width), BF16)]
        + [pack(True, 1)] * core.size,
        inputs + [predict_mine] + predict_others + target_parts + [stream] + embed_held.flat,
        scratch=[pltpu.VMEM((m, part_cols), BF16)],
    )
    stream_others = part.from_others(stream_sum)

    active_on.forward()
    residual_on = Gather(residual_packs[0], residual_packs[1:], True, 1)
    residual_on.join()

    def hidden_rows(ins, outs, _):
        others, matrix = ins[1 : part.size], ins[part.size :]
        grad, mine, sent, rounded_out = outs
        value = added(ins[0], others, half_width)
        grad[...] = value
        rounded = value.astype(BF16)
        back = down_held.to_cols(matrix, rounded)
        mine[...] = back
        sent[...] = back.astype(BF16)
        rounded_out[...] = rounded

    stream_grad, back_mine, back_sum, stream_sent = order.call(
        hidden_rows,
        "hidden",
        [
            struct((m, half_width), F32),
            struct((m, part_cols), F32),
            struct((m, part_cols), BF16),
            struct((m, half_width), BF16),
        ],
        [stream_mine] + stream_others + down_held.flat,
    )
    back_others = wide.from_others(back_sum)
    residual_on.send()
    residual_on.relay()
    order.wait_for(active_on.arrived)

    def normed_rows(ins, outs, _):
        stream_sent, others, matrix = ins[2], ins[3 : 2 + wide.size], ins[2 + wide.size :]
        mine, inner, sent, *packs = outs
        preact = ins[0][...]
        squared, tangent = gelu_parts(preact)
        slope = 0.5 * (1.0 + tangent) + 0.5 * preact * (1.0 - tangent * tangent) * GELU_FACTOR * (
            1.0 + 3.0 * 0.044715 * squared
        )
        value = (added(ins[1], others, part_cols) * slope).astype(BF16)
        for k in range(core.size):
            packs[k][:, :own_cols] = value[:, core_slot(k)]
            packs[k][:, own_cols:] = stream_sent[...]
        grad = up_held.to_width(matrix, value)
        mine[...] = grad
        both = jnp.sum(value.astype(F32) * preact, axis=1, keepdims=True)
        inner[...] = jnp.broadcast_to(both, inner.shape)
        sent[...] = with_scalars(grad, both)

    normed_mine, inner_mine, normed_sum, *hidden_packs = order.call(
        normed_rows,
        "normed",
        [
            struct((m, half_width), F32),
            struct((m, LANES), F32),
            struct((m, half_width + LANES), BF16),
        ]
        + [pack(True, 1)] * core.size,
        [hidden_pre, back_mine, stream_sent] + back_others + up_held.flat,
    )
    normed_others = part.from_others(normed_sum)
    residual_on.forward()
    hidden_on = Gather(hidden_packs[0], hidden_packs[1:], True, 1)
    hidden_on.join()

    def embed_grad_rows(ins, outs, _):
        value, grad, scale_ref, mine, inner_ref, *others = ins
        normed_grad = added(mine, others, half_width)
        inner = inner_ref[:, :1]
        for ref in others:
            inner = inner + scalars_of(ref)
        recip = scale_ref[:, :1]
        outs[0][...] = (
            grad[...] + recip * normed_grad - value[...] * (recip * recip) * (inner / width)
        ).astype(BF16)

    (embed_sent,) = order.call(
        embed_grad_rows,
        "embed_grad",
        [pack(False, 1)],
        [embedded, stream_grad, scale, normed_mine, inner_mine] + normed_others,
    )
    hidden_on.send()
    hidden_on.forward(False)
    embed_sent_on = Gather(embed_sent, [embed_sent] * (core.size - 1), False, 1)
    embed_sent_on.join()
    order.run("join")
    embed_sent_on.send()
    embed_sent_on.forward(False)
    state_out = selected_state(final_cells, arrived_cells)

    def updated(name, terms, momentum, weight, index, begun=()):
        pieces = {}
        for pair in terms:
            for arrays, _ in pair:
                for array in arrays:
                    pieces.setdefault(id(array), array)
        places = {key: place for place, key in enumerate(pieces)}
        arrays = list(pieces.values())
        cuts = 2
        step = own_rows // cuts

        def body(ins, outs, scratch):
            mom_new, weight_new, sems = scratch
            total = None
            for (lefts, left_col), (rights, right_col) in terms:
                for left, right in zip(lefts, rights):
                    left_ref, right_ref = ins[places[id(left)]], ins[places[id(right)]]
                    term = cols_dot(
                        left_ref[:, left_col : left_col + own_rows],
                        right_ref[:, right_col : right_col + own_cols],
                    )
                    total = term if total is None else total + term
            mom, old = ins[len(arrays)], ins[len(arrays) + 1]
            copies = []
            for cut in range(cuts):
                rows = slice(cut * step, (cut + 1) * step)
                fresh = MOMENTUM_DECAY * mom[index][rows] + total[rows]
                mom_new[rows, :] = fresh
                weight_new[rows, :] = (old[index][rows].astype(F32) - LEARNING_RATE * fresh).astype(
                    BF16
                )
                for number, source in enumerate((mom_new, weight_new)):
                    copies.append(
                        pltpu.make_async_copy(
                            source.at[pl.ds(cut * step, step)],
                            outs[number].at[index].at[pl.ds(cut * step, step)],
                            sems.at[2 * cut + number],
                        )
                    )
                    copies[-1].start()
            for copy in copies:
                copy.wait()

        count = len(arrays) + 2
        return order.call(
            body,
            name,
            [struct(momentum.shape, F32), struct(weight.shape, BF16)],
            arrays + [momentum, weight],
            in_hbm=(0, 1),
            scratch=[
                pltpu.VMEM((own_rows, own_cols), F32),
                pltpu.VMEM((own_rows, own_cols), BF16),
                pltpu.SemaphoreType.DMA((2 * cuts,)),
            ],
            aliases={count: 0, count + 1: 1} if begun else None,
            extra=begun,
        )

    all_inputs, all_active, all_residual = (
        inputs_on.pieces(),
        active_on.pieces(),
        residual_on.pieces(),
    )
    all_hidden, all_embed_sent = hidden_on.pieces(), embed_sent_on.pieces()
    begun = updated("update_down", [((all_hidden, own_cols), (all_active, 0))], mom_mlp, mlp, (0, 1))
    mom_mlp_out, mlp_out = updated(
        "update_up", [((all_active, own_cols), (all_hidden, 0))], mom_mlp, mlp, (0, 0), begun
    )
    mom_embed_out, embed_out = updated(
        "update_embed",
        [((all_residual, own_cols), (all_residual, 0)), ((all_embed_sent, 0), (all_inputs, 0))],
        mom_embed,
        embed,
        0,
    )
    return (state_out, embed_out, mlp_out, mom_embed_out, mom_mlp_out)


def solution(mesh):
    placed = (
        P("role", None, None, "dp", "mp"),
        P("role", "dp", "mp"),
        P("role", None, "dp", "mp"),
        P("role", "dp", "mp"),
        P("role", None, "dp", "mp"),
    )
    return jax.shard_map(
        shards,
        mesh=mesh,
        in_specs=placed,
        out_specs=(
            P(None, None, "dp", "mp"),
            P("role", "dp", "mp"),
            P("role", None, "dp", "mp"),
            P("role", "dp", "mp"),
            P("role", None, "dp", "mp"),
        ),
        check_vma=False,
    )
```

```python
import jax
import jax.numpy as jnp
from jax import lax
from jax.experimental import pallas as pl
from jax.experimental.pallas import tpu as pltpu
from jax.sharding import PartitionSpec as P

PATCH = 16
STEPS = 4


SUBSTRATE_DIFFUSION = 0.2
CATALYST_DIFFUSION = 0.1
FEED_RATE = 0.037
KILL_RATE = 0.06
TIME_STEP = 0.8
GELU_FACTOR = 0.7978845608028654
MOMENTUM_DECAY = 0.9
LEARNING_RATE = 0.003

SOLVER, TRAINER = 0, 1
BF16 = jnp.bfloat16
F32 = jnp.float32


class Digit:
    def __init__(self, axis, stride, size):
        self.axis, self.stride, self.size = axis, stride, size

    def shifted(self, value, step):
        pairs = []
        for index in range(lax.axis_size(self.axis)):
            digit = index // self.stride % self.size
            pairs.append((index, index + ((digit + step) % self.size - digit) * self.stride))
        return lax.ppermute(value, self.axis, pairs)

    def from_others(self, value):
        return [self.shifted(value, k) for k in range(1, self.size)]


def rows_dot(left, right):
    return lax.dot_general(left, right, (((1,), (1,)), ((), ())), preferred_element_type=F32)


def cols_dot(left, right):
    return lax.dot_general(left, right, (((0,), (0,)), ((), ())), preferred_element_type=F32)


def dot(left, right):
    return jnp.dot(left, right, preferred_element_type=F32)


def struct(shape, dtype):
    return jax.ShapeDtypeStruct(shape, dtype)


TOKEN = (8, 128)
CHEAP = pl.CostEstimate(flops=1, transcendentals=0, bytes_accessed=1)


class Work:
    def __init__(self, body, outs, args, in_hbm=(), scratch=(), aliases=None, extra=(), left=()):
        self.body, self.outs, self.args = body, list(outs), list(args)
        self.in_hbm, self.scratch, self.aliases = in_hbm, list(scratch), aliases or {}
        self.extra, self.left, self.results = list(extra), left, None


class Order:
    def __init__(self):
        self.token, self.pending, self.riders = None, [], []

    def wait_for(self, arrays):
        self.pending = self.pending + list(arrays)

    def ride(self, *args, **kwargs):
        self.riders.append(Work(*args, **kwargs))
        return self.riders[-1]

    def run(self, name):
        last = self.riders.pop()
        last.results = self.call(
            last.body,
            name,
            last.outs,
            last.args,
            in_hbm=last.in_hbm,
            scratch=last.scratch,
            left=last.left,
        )

    def call(self, body, name, outs, args, **kwargs):
        works = self.riders + [Work(body, outs, args, **kwargs)]
        after = ([] if self.token is None else [self.token]) + self.pending
        self.pending, self.riders = [], []
        vmem, anywhere = pl.BlockSpec(memory_space=pltpu.VMEM), pl.BlockSpec(memory_space=pl.ANY)
        hbm = pl.BlockSpec(memory_space=pltpu.HBM)
        args, in_specs, outs, out_specs, scratch, aliases, room = [], [], [], [], [], {}, 0
        spans = []
        for work in works:
            spans.append((len(args), len(outs), len(scratch)))
            for index, target in work.aliases.items():
                aliases[len(args) + index] = len(outs) + target
            for k, value in enumerate(work.args):
                in_specs.append(hbm if k in work.left else vmem)
                if k in work.left:
                    work.args[k] = pltpu.with_memory_space_constraint(value, pltpu.HBM)
                room += 0 if k in work.left else value.size * value.dtype.itemsize
            for k, value in enumerate(work.outs):
                out_specs.append(hbm if k in work.in_hbm else vmem)
                room += 0 if k in work.in_hbm else value.size * value.dtype.itemsize
            in_specs += [hbm] * len(work.extra)
            args += work.args + work.extra
            outs += work.outs
            scratch += work.scratch
        in_count, out_count = len(args) + len(after), len(outs) + 1

        def kernel(*refs):
            ins, outs_refs, scratch_refs = (
                refs[:in_count],
                refs[in_count : in_count + out_count],
                refs[in_count + out_count :],
            )
            outs_refs[-1][...] = jnp.zeros(TOKEN, F32)
            for work, (first, out, extra) in zip(works, spans):
                work.body(
                    ins[first : first + len(work.args)],
                    outs_refs[out : out + len(work.outs)],
                    scratch_refs[extra : extra + len(work.scratch)],
                )

        *results, self.token = pl.pallas_call(
            kernel,
            name=name,
            out_shape=outs + [struct(TOKEN, F32)],
            in_specs=in_specs + [anywhere] * len(after),
            out_specs=out_specs + [vmem],
            scratch_shapes=scratch,
            input_output_aliases=aliases,
            compiler_params=pltpu.CompilerParams(
                vmem_limit_bytes=min(56 * 2**20, room + 12 * 2**20)
            ),
            cost_estimate=CHEAP,
        )(*args, *after)
        for work, (_, out, _) in zip(works, spans):
            work.results = results[out : out + len(work.outs)]
        return works[-1].results


class Matrix:
    def __init__(self, pieces):
        self.pieces = pieces
        self.row_count, self.col_count = len(pieces), len(pieces[0])
        self.flat = [piece for row in pieces for piece in row]
        self.rows = sum(row[0].shape[0] for row in pieces)
        self.cols = sum(piece.shape[1] for piece in pieces[0])

    def grid(self, refs):
        return [
            refs[index * self.col_count : (index + 1) * self.col_count]
            for index in range(self.row_count)
        ]

    def to_width(self, refs, value):
        done = []
        for row in self.grid(refs):
            total, first = None, 0
            for ref in row:
                term = rows_dot(value[:, first : first + ref.shape[1]], ref[...])
                total = term if total is None else total + term
                first += ref.shape[1]
            done.append(total)
        return jnp.concatenate(done, axis=1) if len(done) > 1 else done[0]

    def to_cols(self, refs, value):
        done = []
        for col in range(self.col_count):
            total, first = None, 0
            for row in self.grid(refs):
                ref = row[col]
                term = dot(value[:, first : first + ref.shape[0]], ref[...])
                total = term if total is None else total + term
                first += ref.shape[0]
            done.append(total)
        return jnp.concatenate(done, axis=1) if len(done) > 1 else done[0]


LANES = 128


def with_scalars(value, column):
    high = column.astype(BF16).astype(F32)
    low = column - high
    lane = lax.broadcasted_iota(jnp.int32, (value.shape[0], LANES), 1)
    extra = jnp.where(lane == 0, high, jnp.where(lane == 1, low, 0.0))
    return jnp.concatenate([value.astype(BF16), extra.astype(BF16)], axis=1)


def scalars_of(received):
    extra = received[:, received.shape[1] - LANES :].astype(F32)
    return jnp.sum(extra, axis=1, keepdims=True)


def swapped_tiles(cells):
    count = cells.shape[0]
    row = lax.broadcasted_iota(jnp.int32, cells.shape, 0)
    run = lax.broadcasted_iota(jnp.int32, cells.shape, 1) // PATCH
    for bit in (1, 2, 4):
        row_set, run_set = (row & bit) != 0, (run & bit) != 0
        moved = jnp.where(
            row_set, pltpu.roll(cells, bit, 0), pltpu.roll(cells, count - bit, 0)
        )
        shift = bit * PATCH
        moved = jnp.where(
            run_set, pltpu.roll(moved, shift, 1), pltpu.roll(moved, LANES - shift, 1)
        )
        cells = jnp.where(row_set == run_set, cells, moved)
    return cells


def write_patches(tile, outs):
    bands = len(outs)
    species, planes = tile.counts
    for s in range(species):
        for p in range(planes):
            plane = swapped_tiles(tile(s, p))
            octets = PATCH // 8
            groups = plane.shape[0] // PATCH
            each = groups // bands
            for o in range(octets):
                col = ((s * planes + p) * octets + o) * LANES
                for index, out in enumerate(outs):
                    rows = [
                        plane[(g * octets + o) * 8 : (g * octets + o + 1) * 8]
                        for g in range(index * each, (index + 1) * each)
                    ]
                    out[:, col : col + LANES] = jnp.concatenate(rows, axis=0).astype(BF16)


class Tile:
    def __init__(self, read, counts):
        self.read, self.counts = read, counts

    def __call__(self, s, p):
        return self.read(s, p)


def packed_edges(order, cells, head_rows, tail_rows, width):
    species, planes, rows, _ = cells.shape
    tall = rows + 2 * width

    def body(ins, outs, _):
        middle, head, tail = ins
        lane = lax.broadcasted_iota(jnp.int32, (tall, LANES), 1)
        total = jnp.zeros((tall, LANES), F32)
        for s in range(species):
            for p in range(planes):
                plane = jnp.concatenate([head[s, p], middle[s, p], tail[s, p]], axis=0)
                slot = (s * planes + p) * width
                first = plane if slot == 0 else pltpu.roll(plane, slot, 1)
                last = pltpu.roll(plane, (LANES // 2 + slot + width) % LANES, 1)
                total = jnp.where((lane >= slot) & (lane < slot + width), first, total)
                start = LANES // 2 + slot
                total = jnp.where((lane >= start) & (lane < start + width), last, total)
        outs[0][...] = total

    return order.ride(body, [struct((tall, LANES), F32)], [cells, head_rows, tail_rows])


def stepped(order, cells, head_rows, tail_rows, from_left, from_right, width, halves):
    species, planes, rows, cols = cells.shape
    tall = rows + 2 * width
    patch_rows = rows // PATCH * (cols // PATCH) // halves
    features = species * planes * PATCH * PATCH

    def body(ins, outs, scratch):
        middle, head, tail, left, right = ins
        (final, *patches), (now, later) = outs, scratch
        lane = lax.broadcasted_iota(jnp.int32, (tall, LANES), 1)
        from_l, from_r = left[...], right[...]
        for s in range(species):
            for p in range(planes):
                slot = (s * planes + p) * width
                now[0, s, p] = jnp.concatenate([head[s, p], middle[s, p], tail[s, p]], axis=0)
                ahead = from_r if slot == 0 else pltpu.roll(from_r, LANES - slot, 1)
                behind = pltpu.roll(from_l, LANES // 2 - slot - width, 1)
                halo = jnp.where(lane < width, ahead, 0.0)
                now[1, s, p] = jnp.where(lane >= LANES - width, behind, halo)

        def neighbours(field, halo):
            up_f, down_f = pltpu.roll(field, 1, 0), pltpu.roll(field, tall - 1, 0)
            up_h, down_h = pltpu.roll(halo, 1, 0), pltpu.roll(halo, tall - 1, 0)
            before_f, before_h = pltpu.roll(field, 1, 1), pltpu.roll(halo, 1, 1)
            after_f, after_h = pltpu.roll(field, LANES - 1, 1), pltpu.roll(halo, LANES - 1, 1)
            first, last = lane == 0, lane == LANES - 1
            sum_f = up_f + down_f + jnp.where(first, before_h, before_f)
            sum_f = sum_f + jnp.where(last, after_h, after_f)
            sum_h = up_h + down_h + jnp.where(first, before_f, before_h)
            sum_h = sum_h + jnp.where(last, after_f, after_h)
            return sum_f, sum_h

        for step in range(STEPS):
            source, target = (now, later) if step % 2 == 0 else (later, now)

            def one_plane(p, carry):
                below, above = jnp.maximum(p - 1, 0), jnp.minimum(p + 1, planes - 1)
                beside = [neighbours(source[0, s, p], source[1, s, p]) for s in range(2)]
                for layer in range(2):
                    u, v = source[layer, 0, p], source[layer, 1, p]
                    lap = []
                    for s, centre in ((0, u), (1, v)):
                        total = source[layer, s, below] + source[layer, s, above]
                        lap.append(total + beside[s][layer] - 6.0 * centre)
                    growth = u * v * v
                    target[layer, 0, p] = u + TIME_STEP * (
                        SUBSTRATE_DIFFUSION * lap[0] - growth + FEED_RATE * (1.0 - u)
                    )
                    target[layer, 1, p] = v + TIME_STEP * (
                        CATALYST_DIFFUSION * lap[1] + growth - (FEED_RATE + KILL_RATE) * v
                    )
                return carry

            lax.fori_loop(0, planes, one_plane, 0)
        source = now if STEPS % 2 == 0 else later
        for s in range(species):
            for p in range(planes):
                final[s, p] = source[0, s, p, width : width + rows]
        write_patches(Tile(lambda s, p: final[s, p], (species, planes)), patches)

    return order.call(
        body,
        "stencil",
        [struct(cells.shape, F32)] + [struct((patch_rows, features), BF16)] * halves,
        [cells, head_rows, tail_rows, from_left, from_right],
        scratch=[pltpu.VMEM((2, species, planes, tall, LANES), F32)] * 2,
    )


def gelu_parts(preact):
    squared = preact * preact
    tangent = jnp.tanh(GELU_FACTOR * (preact + 0.044715 * preact * squared))
    return squared, tangent


def shards(state, embed, mlp, mom_embed, mom_mlp):
    dp_count, mp_count = lax.axis_size("dp"), lax.axis_size("mp")
    halves = 2 if dp_count % 2 == 0 else 1
    pairs = 2 if mp_count % 2 == 0 else 1
    wide = Digit("dp", dp_count // halves, halves)
    band = Digit("dp", 1, dp_count // halves)
    part = Digit("mp", pairs, mp_count // pairs)
    core = Digit("mp", 1, pairs)
    role = Digit("role", 1, lax.axis_size("role"))
    width = embed.shape[1] * dp_count
    own_rows, own_cols = embed.shape[1], embed.shape[2]
    half_width, part_cols = own_rows * band.size, own_cols * core.size
    to_solver, to_trainer = [(TRAINER, SOLVER)], [(SOLVER, TRAINER)]
    order = Order()

    def keep_arrived(arrived, own, index, following, next_index):
        def body(ins, outs, scratch):
            (sems,) = scratch
            solving = lax.axis_index("role") == SOLVER
            if following is not None:
                ahead = pltpu.make_async_copy(ins[2].at[next_index], outs[1], sems.at[0])
                ahead.start()

            @pl.when(solving)
            def _():
                outs[0][...] = ins[0][...]

            @pl.when(jnp.logical_not(solving))
            def _():
                mine = pltpu.make_async_copy(ins[1].at[index], outs[0], sems.at[1])
                mine.start()
                mine.wait()

            if following is not None:
                ahead.wait()

        more = [] if following is None else [following]
        return order.call(
            body,
            "held",
            [struct(arrived.shape, BF16)] * (1 + len(more)),
            [arrived, own] + more,
            left=(1, 2),
            scratch=[pltpu.SemaphoreType.DMA((2,))],
        )

    def relayed(blocks):
        def body(ins, outs, _):
            for source, target in zip(ins, outs):
                target[...] = source[...]

        return order.ride(body, [struct(v.shape, v.dtype) for v in blocks], blocks)

    def own_pieces(block):
        return [block] + core.from_others(block), band.from_others(block)

    def merged(parts):
        return [jnp.concatenate(parts, axis=0)] if len(parts) > 1 else parts

    def held_matrix(own, relay):
        return Matrix([own] + [[rows] + core.from_others(rows) for rows in relay.results])

    cells = state[0]
    rows_in = cells.shape[2]
    features = cells.shape[0] * cells.shape[1] * PATCH * PATCH
    half_rows = rows_in // PATCH * (cells.shape[3] // PATCH) // 2

    def around(axis, step):
        count = lax.axis_size(axis)
        return [(i, (i + step) % count) for i in range(count)]

    def patches_of(ins, outs, _):
        counts = (cells.shape[0], cells.shape[1])
        write_patches(Tile(lambda s, p: ins[0][s, p], counts), outs[:2])
        outs[2][...] = ins[0][:, :, :STEPS]
        outs[3][...] = ins[0][:, :, rows_in - STEPS :]
        outs[4][...] = ins[0][...]

    def split_patches(own, arrived):
        def body(ins, outs, _):
            solving = lax.axis_index("role") == SOLVER
            position = lax.axis_index("mp")
            my_part, my_core = position // core.size, position % core.size
            for k in range(part.size):
                for t in range(core.size):
                    quarter = (my_part + k) % part.size * core.size
                    quarter = quarter + (my_core - t + core.size) % core.size
                    source = pl.ds(pl.multiple_of(quarter * own_cols, own_cols), own_cols)
                    cols = slice(t * own_cols, (t + 1) * own_cols)

                    @pl.when(solving)
                    def _():
                        outs[k][:, cols] = ins[0][:, source]

                    @pl.when(jnp.logical_not(solving))
                    def _():
                        outs[k][:, cols] = ins[1][:, source]

        return order.ride(
            body, [struct((half_rows, part_cols), BF16)] * part.size, [own, arrived]
        )

    def to_parts(cuts):
        return [cuts[0]] + [part.shifted(cuts[k], k) for k in range(1, part.size)]

    def slots(position, size, count):
        for k in range(size):
            slot = (position - k + size) % size
            yield k, pl.ds(pl.multiple_of(slot * count, count), count)

    def order_rows(pieces):
        def body(ins, outs, _):
            for k, rows in slots(lax.axis_index("mp") // core.size, part.size, half_rows):
                outs[0][rows, :] = ins[k][...]

        return order.ride(body, [struct((half_rows * part.size, part_cols), BF16)], pieces)

    def widened(rows):
        return [rows] + wide.from_others(rows)

    def pack(has_features, width_count):
        return struct((m, (own_cols if has_features else 0) + width_count * half_width), BF16)

    class Gather:
        def __init__(self, keep, sends, has_features, width_count):
            self.base = own_cols if has_features else 0
            self.width_count = width_count
            self.parts = [keep] + [core.shifted(sends[k - 1], k) for k in range(1, core.size)]

        def join(self):
            count = band.size if self.width_count else 1
            base = self.base

            def body(ins, outs, _):
                for c, ref in enumerate(ins):
                    rows = slice(c * m, (c + 1) * m)
                    for k in range(count):
                        if base:
                            outs[k][rows, :base] = ref[:, :base]
                        for index in range(self.width_count):
                            first = base + index * half_width + (-k) % band.size * own_rows
                            target = base + index * own_rows
                            outs[k][rows, target : target + own_rows] = ref[
                                :, first : first + own_rows
                            ]

            cols = base + self.width_count * own_rows
            self.joining = order.ride(
                body, [struct((m * core.size, cols), BF16)] * count, self.parts
            )

        def join_for_role(self):
            self.join()

            def body(ins, outs, _):
                for c, ref in enumerate(ins):
                    outs[0][c * m : (c + 1) * m, :] = ref[...]

            cols = self.base + self.width_count * half_width
            self.whole = order.ride(body, [struct((m * core.size, cols), BF16)], self.parts)

        def send_role_first(self):
            (whole,) = self.whole.results
            cuts = self.joining.results
            self.kept = cuts[0]
            self.banded = merged(
                [band.shifted(cuts[k % len(cuts)], k) for k in range(1, band.size)]
            )
            self.crossed = role.from_others(whole)

        def cut_crossed(self):
            base = self.base

            def body(ins, outs, _):
                for number, ref in enumerate(ins):
                    for k in range(band.size):
                        out = outs[number * band.size + k]
                        out[:, :base] = ref[:, :base]
                        for index in range(self.width_count):
                            first = base + index * half_width + (-k) % band.size * own_rows
                            target = base + index * own_rows
                            out[:, target : target + own_rows] = ref[:, first : first + own_rows]

            cols = base + self.width_count * own_rows
            self.cutting = order.ride(
                body,
                [struct((m * core.size, cols), BF16)] * (band.size * len(self.crossed)),
                self.crossed,
            )

        def band_crossed(self):
            self.arrived = []
            cuts = self.cutting.results
            for number in range(len(self.crossed)):
                own = cuts[number * band.size : (number + 1) * band.size]
                self.arrived += [own[0]] + merged(
                    [band.shifted(own[k], k) for k in range(1, band.size)]
                )

        def send(self):
            cuts = self.joining.results
            self.kept = cuts[0]
            self.banded = merged(
                [band.shifted(cuts[k % len(cuts)], k) for k in range(1, band.size)]
            )
            self.arrived = role.from_others(self.kept)

        def relay(self):
            self.relaying = relayed(self.banded)

        def forward(self, relayed_too=True):
            self.banded = self.relaying.results if relayed_too else self.banded
            for piece in self.banded:
                self.arrived = self.arrived + role.from_others(piece)

        def pieces(self):
            return [self.kept] + self.banded + self.arrived

    def product(lefts, left_col, rights, right_col):
        total = None
        for left, right in zip(lefts, rights):
            term = cols_dot(
                left[:, left_col : left_col + own_rows], right[:, right_col : right_col + own_cols]
            )
            total = term if total is None else total + term
        return total

    def begun_gradient(lefts, left_col, rights, right_col):
        count = len(lefts)

        def body(ins, outs, _):
            outs[0][...] = product(ins[:count], left_col, ins[count:], right_col)

        return order.ride(body, [struct((own_rows, own_cols), F32)], lefts + rights)

    def selected_state(own, arrived):
        def body(ins, outs, scratch):
            solving = lax.axis_index("role") == SOLVER
            (sem,) = scratch
            for chosen, source in ((solving, ins[0]), (jnp.logical_not(solving), ins[1])):

                @pl.when(chosen)
                def _():
                    copy = pltpu.make_async_copy(source, outs[0], sem)
                    copy.start()
                    copy.wait()

        scratch = [pltpu.SemaphoreType.DMA]
        outs = [struct(own.shape, F32)]
        return order.call(body, "state", outs, [own, arrived], in_hbm=(0,), scratch=scratch)[0]

    m = half_rows * part.size * wide.size
    total_rows = m * core.size * band.size * role.size
    loss_scale = float(total_rows) ** (-0.5)

    arrived_embed = lax.ppermute(embed[0], "role", to_solver)
    edge_struct = struct(cells.shape[:2] + (STEPS, cells.shape[3]), F32)
    *start_halves, first_rows, last_rows, cells = order.call(
        patches_of,
        "patches",
        [struct((half_rows, features), BF16)] * 2 + [edge_struct] * 2 + [struct(cells.shape, F32)],
        [cells],
    )
    arrived_start = lax.ppermute(start_halves[1], "role", to_trainer)
    head_rows = lax.ppermute(last_rows, "dp", around("dp", 1))
    tail_rows = lax.ppermute(first_rows, "dp", around("dp", -1))
    splitting = split_patches(start_halves[0], arrived_start)
    order.wait_for([head_rows, tail_rows])
    order.run("split")
    embed_kept, up_block = keep_arrived(arrived_embed, embed, 0, mlp, (0, 0))
    embed_own, embed_bands = own_pieces(embed_kept)
    arrived_up = lax.ppermute(up_block, "role", to_solver)
    ordering = order_rows(to_parts(splitting.results))
    edging = packed_edges(order, cells, head_rows, tail_rows, STEPS)
    order.run("order")
    input_parts = widened(*ordering.results)
    (edges,) = edging.results
    from_left = lax.ppermute(edges, "mp", around("mp", 1))
    from_right = lax.ppermute(edges, "mp", around("mp", -1))
    relay = relayed(merged(embed_bands))
    order.wait_for([from_left, from_right] + input_parts[1:])
    up_kept, down_block = keep_arrived(arrived_up, mlp, (0, 0), mlp, (0, 1))
    up_own, up_bands = own_pieces(up_kept)
    arrived_down = lax.ppermute(down_block, "role", to_solver)
    embed_held = held_matrix(embed_own, relay)

    def embed_rows(ins, outs, _):
        parts, matrix = ins[: wide.size], ins[wide.size :]
        *inputs, mine, sent = outs
        position = lax.axis_index("dp") // band.size
        for k, rows in slots(position, wide.size, half_rows * part.size):
            for t in range(core.size):
                inputs[t][rows, :] = parts[k][:, t * own_cols : (t + 1) * own_cols]
        value = embed_held.to_width(matrix, jnp.concatenate([ref[...] for ref in inputs], axis=1))
        mine[...] = value
        sent[...] = value.astype(BF16)

    *inputs, embed_mine, embed_sum = order.call(
        embed_rows,
        "embed",
        [struct((m, own_cols), BF16)] * core.size
        + [struct((m, half_width), F32), struct((m, half_width), BF16)],
        input_parts + embed_held.flat,
    )
    embed_others = part.from_others(embed_sum)

    def core_slot(k):
        return slice((-k) % core.size * own_cols, ((-k) % core.size + 1) * own_cols)

    final_cells, *end_halves = stepped(
        order, cells, head_rows, tail_rows, from_left, from_right, STEPS, 2
    )
    (arrived_end,) = role.from_others(end_halves[1])
    relay = relayed(merged(up_bands))
    order.wait_for(embed_others)
    (down_kept,) = keep_arrived(arrived_down, mlp, (0, 1), None, ())
    down_own, down_bands = own_pieces(down_kept)
    up_held = held_matrix(up_own, relay)
    copying = relayed([final_cells])

    def added(mine, refs, cols):
        total = mine[...]
        for ref in refs:
            total = total + ref[:, :cols].astype(F32)
        return total

    def up_rows(ins, outs, _):
        others, matrix = ins[1 : part.size], ins[part.size :]
        embedded, mine, sent = outs
        value = added(ins[0], others, half_width)
        embedded[...] = value
        hidden = up_held.to_cols(matrix, value.astype(BF16))
        mine[...] = hidden
        sent[...] = with_scalars(hidden, jnp.sum(value * value, axis=1, keepdims=True))

    embedded, up_mine, up_sum = order.call(
        up_rows,
        "up",
        [
            struct((m, half_width), F32),
            struct((m, part_cols), F32),
            struct((m, part_cols + LANES), BF16),
        ],
        [embed_mine] + embed_others + up_held.flat,
    )
    up_others = wide.from_others(up_sum)
    (arrived_cells,) = role.from_others(copying.results[0])
    order.wait_for(up_others + [arrived_cells])
    splitting = split_patches(end_halves[0], arrived_end)
    inputs_on = Gather(inputs[0], [inputs[(-k) % core.size] for k in range(1, core.size)], True, 0)
    inputs_on.join()
    relay = relayed(merged(down_bands))
    order.run("relay")
    down_held = held_matrix(down_own, relay)
    target_cuts = to_parts(splitting.results)
    inputs_on.send()

    def down_rows(ins, outs, _):
        value, others, matrix = ins[0][...], ins[2 : 1 + wide.size], ins[1 + wide.size :]
        hidden, mine, sent, scale, *packs = outs
        squares = jnp.sum(value * value, axis=1, keepdims=True)
        for ref in others:
            squares = squares + scalars_of(ref)
        recip = lax.rsqrt(squares / width + 1e-06)
        preact = added(ins[1], others, part_cols) * recip
        hidden[...] = preact
        normed = (value * recip).astype(BF16)
        _, tangent = gelu_parts(preact)
        active = (0.5 * preact * (1.0 + tangent)).astype(BF16)
        branch = down_held.to_width(matrix, active)
        mine[...] = branch
        sent[...] = branch.astype(BF16)
        scale[...] = jnp.broadcast_to(recip, scale.shape)
        for k in range(core.size):
            packs[k][:, :own_cols] = active[:, core_slot(k)]
            packs[k][:, own_cols:] = normed

    hidden_pre, down_mine, down_sum, scale, *active_packs = order.call(
        down_rows,
        "down",
        [
            struct((m, part_cols), F32),
            struct((m, half_width), F32),
            struct((m, half_width), BF16),
            struct((m, LANES), F32),
        ]
        + [pack(True, 1)] * core.size,
        [embedded, up_mine] + up_others + down_held.flat,
    )
    down_others = part.from_others(down_sum)
    active_on = Gather(active_packs[0], active_packs[1:], True, 1)
    active_on.join()
    inputs_on.relay()
    order.wait_for(inputs_on.arrived)

    def predict_rows(ins, outs, _):
        aims, ins = ins[: part.size], ins[part.size :]
        others, matrix = ins[2 : 1 + part.size], ins[1 + part.size :]
        mine, sent, stream = outs
        value = (ins[0][...] + added(ins[1], others, half_width)).astype(BF16)
        stream[...] = value
        mine[...] = embed_held.to_cols(matrix, value)
        position = lax.axis_index("dp") // band.size * part.size
        for k, ref in enumerate(aims):
            slot = (lax.axis_index("mp") // core.size - k + part.size) % part.size
            rows = pl.ds(pl.multiple_of((position + slot) * half_rows, half_rows), half_rows)
            mine[rows, :] = mine[rows, :] - ref[...].astype(F32)
        sent[...] = mine[...].astype(BF16)

    predict_mine, predict_sum, stream = order.call(
        predict_rows,
        "predict",
        [
            struct((m, part_cols), F32),
            struct((m, part_cols), BF16),
            struct((m, half_width), BF16),
        ],
        target_cuts + [embedded, down_mine] + down_others + embed_held.flat,
    )
    predict_others = wide.from_others(predict_sum)
    inputs_on.forward()
    active_on.send()
    active_on.relay()
    order.wait_for(inputs_on.arrived + active_on.arrived)

    def residual_rows(ins, outs, _):
        inputs, ins = ins[: core.size], ins[core.size :]
        mine_in, others, ins = ins[0], ins[1 : wide.size], ins[wide.size :]
        stream, matrix = ins[0], ins[1:]
        mine, sent, *packs = outs
        known = jnp.concatenate([ref[...] for ref in inputs], axis=1).astype(F32)
        value = ((known + added(mine_in, others, part_cols)) * loss_scale).astype(BF16)
        for k in range(core.size):
            packs[k][:, :own_cols] = value[:, core_slot(k)]
            packs[k][:, own_cols:] = stream[...]
        grad = embed_held.to_width(matrix, value)
        mine[...] = grad
        sent[...] = grad.astype(BF16)

    stream_mine, stream_sum, *residual_packs = order.call(
        residual_rows,
        "residual",
        [struct((m, half_width), F32), struct((m, half_width), BF16)]
        + [pack(True, 1)] * core.size,
        inputs + [predict_mine] + predict_others + [stream] + embed_held.flat,
    )
    stream_others = part.from_others(stream_sum)

    active_on.forward()
    residual_on = Gather(residual_packs[0], residual_packs[1:], True, 1)
    residual_on.join_for_role()

    def hidden_rows(ins, outs, _):
        others, matrix = ins[1 : part.size], ins[part.size :]
        grad, mine, sent, rounded_out = outs
        value = added(ins[0], others, half_width)
        grad[...] = value
        rounded = value.astype(BF16)
        back = down_held.to_cols(matrix, rounded)
        mine[...] = back
        sent[...] = back.astype(BF16)
        rounded_out[...] = rounded

    stream_grad, back_mine, back_sum, stream_sent = order.call(
        hidden_rows,
        "hidden",
        [
            struct((m, half_width), F32),
            struct((m, part_cols), F32),
            struct((m, part_cols), BF16),
            struct((m, half_width), BF16),
        ],
        [stream_mine] + stream_others + down_held.flat,
    )
    back_others = wide.from_others(back_sum)
    residual_on.send_role_first()
    order.wait_for(active_on.arrived + residual_on.banded + residual_on.crossed)

    def normed_rows(ins, outs, _):
        stream_sent, others, matrix = ins[2], ins[3 : 2 + wide.size], ins[2 + wide.size :]
        mine, inner, sent, *packs = outs
        preact = ins[0][...]
        squared, tangent = gelu_parts(preact)
        slope = 0.5 * (1.0 + tangent) + 0.5 * preact * (1.0 - tangent * tangent) * GELU_FACTOR * (
            1.0 + 3.0 * 0.044715 * squared
        )
        value = (added(ins[1], others, part_cols) * slope).astype(BF16)
        for k in range(core.size):
            packs[k][:, :own_cols] = value[:, core_slot(k)]
            packs[k][:, own_cols:] = stream_sent[...]
        grad = up_held.to_width(matrix, value)
        mine[...] = grad
        both = jnp.sum(value.astype(F32) * preact, axis=1, keepdims=True)
        inner[...] = jnp.broadcast_to(both, inner.shape)
        sent[...] = with_scalars(grad, both)

    normed_mine, inner_mine, normed_sum, *hidden_packs = order.call(
        normed_rows,
        "normed",
        [
            struct((m, half_width), F32),
            struct((m, LANES), F32),
            struct((m, half_width + LANES), BF16),
        ]
        + [pack(True, 1)] * core.size,
        [hidden_pre, back_mine, stream_sent] + back_others + up_held.flat,
    )
    normed_others = part.from_others(normed_sum)
    hidden_on = Gather(hidden_packs[0], hidden_packs[1:], True, 1)
    hidden_on.join()
    order.run("join")
    hidden_on.send()
    hidden_on.forward(False)
    residual_on.cut_crossed()

    def embed_grad_rows(ins, outs, _):
        value, grad, scale_ref, mine, inner_ref, *others = ins
        normed_grad = added(mine, others, half_width)
        inner = inner_ref[:, :1]
        for ref in others:
            inner = inner + scalars_of(ref)
        recip = scale_ref[:, :1]
        outs[0][...] = (
            grad[...] + recip * normed_grad - value[...] * (recip * recip) * (inner / width)
        ).astype(BF16)

    (embed_sent,) = order.call(
        embed_grad_rows,
        "embed_grad",
        [pack(False, 1)],
        [embedded, stream_grad, scale, normed_mine, inner_mine] + normed_others,
    )
    embed_sent_on = Gather(embed_sent, [embed_sent] * (core.size - 1), False, 1)
    embed_sent_on.join()
    order.run("join")
    embed_sent_on.send()
    embed_sent_on.forward(False)
    residual_on.band_crossed()
    all_residual = residual_on.pieces()
    embed_term = begun_gradient(all_residual, own_cols, all_residual, 0)
    state_out = selected_state(final_cells, arrived_cells)

    def updated(name, lefts, left_col, rights, right_col, momentum, weight, index, term=(), begun=()):
        arrays = lefts + rights + list(term)
        count = len(lefts)
        cuts = 2
        step = own_rows // cuts

        def body(ins, outs, scratch):
            mom_new, weight_new, sems = scratch
            total = product(ins[:count], left_col, ins[count : 2 * count], right_col)
            for ref in ins[2 * count : len(arrays)]:
                total = total + ref[...]
            mom, old = ins[len(arrays)], ins[len(arrays) + 1]
            copies = []
            for cut in range(cuts):
                rows = slice(cut * step, (cut + 1) * step)
                fresh = MOMENTUM_DECAY * mom[index][rows] + total[rows]
                mom_new[rows, :] = fresh
                weight_new[rows, :] = (old[index][rows].astype(F32) - LEARNING_RATE * fresh).astype(
                    BF16
                )
                for number, source in enumerate((mom_new, weight_new)):
                    copies.append(
                        pltpu.make_async_copy(
                            source.at[pl.ds(cut * step, step)],
                            outs[number].at[index].at[pl.ds(cut * step, step)],
                            sems.at[2 * cut + number],
                        )
                    )
                    copies[-1].start()
            for copy in copies:
                copy.wait()

        return order.call(
            body,
            name,
            [struct(momentum.shape, F32), struct(weight.shape, BF16)],
            arrays + [momentum, weight],
            in_hbm=(0, 1),
            scratch=[
                pltpu.VMEM((own_rows, own_cols), F32),
                pltpu.VMEM((own_rows, own_cols), BF16),
                pltpu.SemaphoreType.DMA((2 * cuts,)),
            ],
            aliases={len(arrays) + 2: 0, len(arrays) + 3: 1} if begun else None,
            extra=begun,
        )

    all_inputs, all_active = inputs_on.pieces(), active_on.pieces()
    all_hidden, all_embed_sent = hidden_on.pieces(), embed_sent_on.pieces()
    begun = updated("update_down", all_hidden, own_cols, all_active, 0, mom_mlp, mlp, (0, 1))
    mom_mlp_out, mlp_out = updated(
        "update_up", all_active, own_cols, all_hidden, 0, mom_mlp, mlp, (0, 0), begun=begun
    )
    mom_embed_out, embed_out = updated(
        "update_embed", all_embed_sent, 0, all_inputs, 0, mom_embed, embed, 0, embed_term.results
    )
    return (state_out, embed_out, mlp_out, mom_embed_out, mom_mlp_out)


def solution(mesh):
    placed = (
        P("role", None, None, "dp", "mp"),
        P("role", "dp", "mp"),
        P("role", None, "dp", "mp"),
        P("role", "dp", "mp"),
        P("role", None, "dp", "mp"),
    )
    return jax.shard_map(
        shards,
        mesh=mesh,
        in_specs=placed,
        out_specs=(
            P(None, None, "dp", "mp"),
            P("role", "dp", "mp"),
            P("role", None, "dp", "mp"),
            P("role", "dp", "mp"),
            P("role", None, "dp", "mp"),
        ),
        check_vma=False,
    )
```

```python
import jax
import jax.numpy as jnp
from jax import lax
from jax.experimental import pallas as pl
from jax.experimental.pallas import tpu as pltpu
from jax.sharding import PartitionSpec as P

PATCH = 16
STEPS = 4


SUBSTRATE_DIFFUSION = 0.2
CATALYST_DIFFUSION = 0.1
FEED_RATE = 0.037
KILL_RATE = 0.06
TIME_STEP = 0.8
GELU_FACTOR = 0.7978845608028654
MOMENTUM_DECAY = 0.9
LEARNING_RATE = 0.003

SOLVER, TRAINER = 0, 1
BF16 = jnp.bfloat16
F32 = jnp.float32


class Digit:
    def __init__(self, axis, stride, size):
        self.axis, self.stride, self.size = axis, stride, size

    def shifted(self, value, step):
        pairs = []
        for index in range(lax.axis_size(self.axis)):
            digit = index // self.stride % self.size
            pairs.append((index, index + ((digit + step) % self.size - digit) * self.stride))
        return lax.ppermute(value, self.axis, pairs)

    def from_others(self, value):
        return [self.shifted(value, k) for k in range(1, self.size)]


def rows_dot(left, right):
    return lax.dot_general(left, right, (((1,), (1,)), ((), ())), preferred_element_type=F32)


def cols_dot(left, right):
    return lax.dot_general(left, right, (((0,), (0,)), ((), ())), preferred_element_type=F32)


def dot(left, right):
    return jnp.dot(left, right, preferred_element_type=F32)


def struct(shape, dtype):
    return jax.ShapeDtypeStruct(shape, dtype)


TOKEN = (8, 128)
CHEAP = pl.CostEstimate(flops=1, transcendentals=0, bytes_accessed=1)


class Work:
    def __init__(self, body, outs, args, in_hbm=(), scratch=(), aliases=None, extra=(), left=()):
        self.body, self.outs, self.args = body, list(outs), list(args)
        self.in_hbm, self.scratch, self.aliases = in_hbm, list(scratch), aliases or {}
        self.extra, self.left, self.results = list(extra), left, None


class Order:
    def __init__(self):
        self.token, self.pending, self.riders = None, [], []

    def wait_for(self, arrays):
        self.pending = self.pending + list(arrays)

    def ride(self, *args, **kwargs):
        self.riders.append(Work(*args, **kwargs))
        return self.riders[-1]

    def run(self, name):
        last = self.riders.pop()
        last.results = self.call(
            last.body,
            name,
            last.outs,
            last.args,
            in_hbm=last.in_hbm,
            scratch=last.scratch,
            left=last.left,
        )

    def call(self, body, name, outs, args, **kwargs):
        works = self.riders + [Work(body, outs, args, **kwargs)]
        after = ([] if self.token is None else [self.token]) + self.pending
        self.pending, self.riders = [], []
        vmem, anywhere = pl.BlockSpec(memory_space=pltpu.VMEM), pl.BlockSpec(memory_space=pl.ANY)
        hbm = pl.BlockSpec(memory_space=pltpu.HBM)
        args, in_specs, outs, out_specs, scratch, aliases, room = [], [], [], [], [], {}, 0
        spans = []
        for work in works:
            spans.append((len(args), len(outs), len(scratch)))
            for index, target in work.aliases.items():
                aliases[len(args) + index] = len(outs) + target
            for k, value in enumerate(work.args):
                in_specs.append(hbm if k in work.left else vmem)
                if k in work.left:
                    work.args[k] = pltpu.with_memory_space_constraint(value, pltpu.HBM)
                room += 0 if k in work.left else value.size * value.dtype.itemsize
            for k, value in enumerate(work.outs):
                out_specs.append(hbm if k in work.in_hbm else vmem)
                room += 0 if k in work.in_hbm else value.size * value.dtype.itemsize
            in_specs += [hbm] * len(work.extra)
            args += work.args + work.extra
            outs += work.outs
            scratch += work.scratch
        in_count, out_count = len(args) + len(after), len(outs) + 1

        def kernel(*refs):
            ins, outs_refs, scratch_refs = (
                refs[:in_count],
                refs[in_count : in_count + out_count],
                refs[in_count + out_count :],
            )
            outs_refs[-1][...] = jnp.zeros(TOKEN, F32)
            for work, (first, out, extra) in zip(works, spans):
                work.body(
                    ins[first : first + len(work.args)],
                    outs_refs[out : out + len(work.outs)],
                    scratch_refs[extra : extra + len(work.scratch)],
                )

        *results, self.token = pl.pallas_call(
            kernel,
            name=name,
            out_shape=outs + [struct(TOKEN, F32)],
            in_specs=in_specs + [anywhere] * len(after),
            out_specs=out_specs + [vmem],
            scratch_shapes=scratch,
            input_output_aliases=aliases,
            compiler_params=pltpu.CompilerParams(
                vmem_limit_bytes=min(56 * 2**20, room + 12 * 2**20)
            ),
            cost_estimate=CHEAP,
        )(*args, *after)
        for work, (_, out, _) in zip(works, spans):
            work.results = results[out : out + len(work.outs)]
        return works[-1].results


class Matrix:
    def __init__(self, pieces):
        self.pieces = pieces
        self.row_count, self.col_count = len(pieces), len(pieces[0])
        self.flat = [piece for row in pieces for piece in row]
        self.rows = sum(row[0].shape[0] for row in pieces)
        self.cols = sum(piece.shape[1] for piece in pieces[0])

    def grid(self, refs):
        return [
            refs[index * self.col_count : (index + 1) * self.col_count]
            for index in range(self.row_count)
        ]

    def to_width(self, refs, value):
        done = []
        for row in self.grid(refs):
            total, first = None, 0
            for ref in row:
                term = rows_dot(value[:, first : first + ref.shape[1]], ref[...])
                total = term if total is None else total + term
                first += ref.shape[1]
            done.append(total)
        return jnp.concatenate(done, axis=1) if len(done) > 1 else done[0]

    def to_cols(self, refs, value):
        done = []
        for col in range(self.col_count):
            total, first = None, 0
            for row in self.grid(refs):
                ref = row[col]
                term = dot(value[:, first : first + ref.shape[0]], ref[...])
                total = term if total is None else total + term
                first += ref.shape[0]
            done.append(total)
        return jnp.concatenate(done, axis=1) if len(done) > 1 else done[0]


LANES = 128


def with_scalars(value, column):
    high = column.astype(BF16).astype(F32)
    low = column - high
    lane = lax.broadcasted_iota(jnp.int32, (value.shape[0], LANES), 1)
    extra = jnp.where(lane == 0, high, jnp.where(lane == 1, low, 0.0))
    return jnp.concatenate([value.astype(BF16), extra.astype(BF16)], axis=1)


def scalars_of(received):
    extra = received[:, received.shape[1] - LANES :].astype(F32)
    return jnp.sum(extra, axis=1, keepdims=True)


def swapped_tiles(cells):
    count = cells.shape[0]
    row = lax.broadcasted_iota(jnp.int32, cells.shape, 0)
    run = lax.broadcasted_iota(jnp.int32, cells.shape, 1) // PATCH
    for bit in (1, 2, 4):
        row_set, run_set = (row & bit) != 0, (run & bit) != 0
        moved = jnp.where(
            row_set, pltpu.roll(cells, bit, 0), pltpu.roll(cells, count - bit, 0)
        )
        shift = bit * PATCH
        moved = jnp.where(
            run_set, pltpu.roll(moved, shift, 1), pltpu.roll(moved, LANES - shift, 1)
        )
        cells = jnp.where(row_set == run_set, cells, moved)
    return cells


def write_patches(tile, outs):
    bands = len(outs)
    species, planes = tile.counts
    for s in range(species):
        for p in range(planes):
            plane = swapped_tiles(tile(s, p))
            octets = PATCH // 8
            groups = plane.shape[0] // PATCH
            each = groups // bands
            for o in range(octets):
                col = ((s * planes + p) * octets + o) * LANES
                for index, out in enumerate(outs):
                    rows = [
                        plane[(g * octets + o) * 8 : (g * octets + o + 1) * 8]
                        for g in range(index * each, (index + 1) * each)
                    ]
                    out[:, col : col + LANES] = jnp.concatenate(rows, axis=0).astype(BF16)


class Tile:
    def __init__(self, read, counts):
        self.read, self.counts = read, counts

    def __call__(self, s, p):
        return self.read(s, p)


def packed_edges(order, cells, head_rows, tail_rows, width):
    species, planes, rows, _ = cells.shape
    tall = rows + 2 * width

    def body(ins, outs, _):
        middle, head, tail = ins
        lane = lax.broadcasted_iota(jnp.int32, (tall, LANES), 1)
        total = jnp.zeros((tall, LANES), F32)
        for s in range(species):
            for p in range(planes):
                plane = jnp.concatenate([head[s, p], middle[s, p], tail[s, p]], axis=0)
                slot = (s * planes + p) * width
                first = plane if slot == 0 else pltpu.roll(plane, slot, 1)
                last = pltpu.roll(plane, (LANES // 2 + slot + width) % LANES, 1)
                total = jnp.where((lane >= slot) & (lane < slot + width), first, total)
                start = LANES // 2 + slot
                total = jnp.where((lane >= start) & (lane < start + width), last, total)
        outs[0][...] = total

    return order.ride(body, [struct((tall, LANES), F32)], [cells, head_rows, tail_rows])


def stepped(order, cells, head_rows, tail_rows, from_left, from_right, width, halves):
    species, planes, rows, cols = cells.shape
    tall = rows + 2 * width
    patch_rows = rows // PATCH * (cols // PATCH) // halves
    features = species * planes * PATCH * PATCH

    def body(ins, outs, scratch):
        middle, head, tail, left, right = ins
        (final, *patches), (now, later) = outs, scratch
        lane = lax.broadcasted_iota(jnp.int32, (tall, LANES), 1)
        from_l, from_r = left[...], right[...]
        for s in range(species):
            for p in range(planes):
                slot = (s * planes + p) * width
                now[0, s, p] = jnp.concatenate([head[s, p], middle[s, p], tail[s, p]], axis=0)
                ahead = from_r if slot == 0 else pltpu.roll(from_r, LANES - slot, 1)
                behind = pltpu.roll(from_l, LANES // 2 - slot - width, 1)
                halo = jnp.where(lane < width, ahead, 0.0)
                now[1, s, p] = jnp.where(lane >= LANES - width, behind, halo)

        def neighbours(field, halo):
            up_f, down_f = pltpu.roll(field, 1, 0), pltpu.roll(field, tall - 1, 0)
            up_h, down_h = pltpu.roll(halo, 1, 0), pltpu.roll(halo, tall - 1, 0)
            before_f, before_h = pltpu.roll(field, 1, 1), pltpu.roll(halo, 1, 1)
            after_f, after_h = pltpu.roll(field, LANES - 1, 1), pltpu.roll(halo, LANES - 1, 1)
            first, last = lane == 0, lane == LANES - 1
            sum_f = up_f + down_f + jnp.where(first, before_h, before_f)
            sum_f = sum_f + jnp.where(last, after_h, after_f)
            sum_h = up_h + down_h + jnp.where(first, before_f, before_h)
            sum_h = sum_h + jnp.where(last, after_f, after_h)
            return sum_f, sum_h

        for step in range(STEPS):
            source, target = (now, later) if step % 2 == 0 else (later, now)

            def one_plane(p, carry):
                below, above = jnp.maximum(p - 1, 0), jnp.minimum(p + 1, planes - 1)
                beside = [neighbours(source[0, s, p], source[1, s, p]) for s in range(2)]
                for layer in range(2):
                    u, v = source[layer, 0, p], source[layer, 1, p]
                    lap = []
                    for s, centre in ((0, u), (1, v)):
                        total = source[layer, s, below] + source[layer, s, above]
                        lap.append(total + beside[s][layer] - 6.0 * centre)
                    growth = u * v * v
                    target[layer, 0, p] = u + TIME_STEP * (
                        SUBSTRATE_DIFFUSION * lap[0] - growth + FEED_RATE * (1.0 - u)
                    )
                    target[layer, 1, p] = v + TIME_STEP * (
                        CATALYST_DIFFUSION * lap[1] + growth - (FEED_RATE + KILL_RATE) * v
                    )
                return carry

            lax.fori_loop(0, planes, one_plane, 0)
        source = now if STEPS % 2 == 0 else later
        for s in range(species):
            for p in range(planes):
                final[s, p] = source[0, s, p, width : width + rows]
        write_patches(Tile(lambda s, p: final[s, p], (species, planes)), patches)

    return order.call(
        body,
        "stencil",
        [struct(cells.shape, F32)] + [struct((patch_rows, features), BF16)] * halves,
        [cells, head_rows, tail_rows, from_left, from_right],
        scratch=[pltpu.VMEM((2, species, planes, tall, LANES), F32)] * 2,
    )


def gelu_parts(preact):
    squared = preact * preact
    tangent = jnp.tanh(GELU_FACTOR * (preact + 0.044715 * preact * squared))
    return squared, tangent


def shards(state, embed, mlp, mom_embed, mom_mlp):
    dp_count, mp_count = lax.axis_size("dp"), lax.axis_size("mp")
    halves = 2 if dp_count % 2 == 0 else 1
    pairs = 2 if mp_count % 2 == 0 else 1
    wide = Digit("dp", dp_count // halves, halves)
    band = Digit("dp", 1, dp_count // halves)
    part = Digit("mp", pairs, mp_count // pairs)
    core = Digit("mp", 1, pairs)
    role = Digit("role", 1, lax.axis_size("role"))
    width = embed.shape[1] * dp_count
    own_rows, own_cols = embed.shape[1], embed.shape[2]
    half_width, part_cols = own_rows * band.size, own_cols * core.size
    to_solver, to_trainer = [(TRAINER, SOLVER)], [(SOLVER, TRAINER)]
    order = Order()

    def keep_arrived(arrived, own, index, following, next_index):
        def body(ins, outs, scratch):
            (sems,) = scratch
            solving = lax.axis_index("role") == SOLVER
            if following is not None:
                ahead = pltpu.make_async_copy(ins[2].at[next_index], outs[1], sems.at[0])
                ahead.start()

            @pl.when(solving)
            def _():
                outs[0][...] = ins[0][...]

            @pl.when(jnp.logical_not(solving))
            def _():
                mine = pltpu.make_async_copy(ins[1].at[index], outs[0], sems.at[1])
                mine.start()
                mine.wait()

            if following is not None:
                ahead.wait()

        more = [] if following is None else [following]
        return order.call(
            body,
            "held",
            [struct(arrived.shape, BF16)] * (1 + len(more)),
            [arrived, own] + more,
            left=(1, 2),
            scratch=[pltpu.SemaphoreType.DMA((2,))],
        )

    def relayed(blocks):
        def body(ins, outs, _):
            for source, target in zip(ins, outs):
                target[...] = source[...]

        return order.ride(body, [struct(v.shape, v.dtype) for v in blocks], blocks)

    def own_pieces(block):
        return [block] + core.from_others(block), band.from_others(block)

    def merged(parts):
        return [jnp.concatenate(parts, axis=0)] if len(parts) > 1 else parts

    def held_matrix(own, relay):
        return Matrix([own] + [[rows] + core.from_others(rows) for rows in relay.results])

    cells = state[0]
    rows_in = cells.shape[2]
    features = cells.shape[0] * cells.shape[1] * PATCH * PATCH
    half_rows = rows_in // PATCH * (cells.shape[3] // PATCH) // 2

    def around(axis, step):
        count = lax.axis_size(axis)
        return [(i, (i + step) % count) for i in range(count)]

    def patches_of(ins, outs, _):
        counts = (cells.shape[0], cells.shape[1])
        write_patches(Tile(lambda s, p: ins[0][s, p], counts), outs[:2])
        outs[2][...] = ins[0][:, :, :STEPS]
        outs[3][...] = ins[0][:, :, rows_in - STEPS :]
        outs[4][...] = ins[0][...]

    def split_patches(own, arrived):
        def body(ins, outs, _):
            solving = lax.axis_index("role") == SOLVER
            position = lax.axis_index("mp")
            my_part, my_core = position // core.size, position % core.size
            for k in range(part.size):
                for t in range(core.size):
                    quarter = (my_part + k) % part.size * core.size
                    quarter = quarter + (my_core - t + core.size) % core.size
                    source = pl.ds(pl.multiple_of(quarter * own_cols, own_cols), own_cols)
                    cols = slice(t * own_cols, (t + 1) * own_cols)

                    @pl.when(solving)
                    def _():
                        outs[k][:, cols] = ins[0][:, source]

                    @pl.when(jnp.logical_not(solving))
                    def _():
                        outs[k][:, cols] = ins[1][:, source]

        return order.ride(
            body, [struct((half_rows, part_cols), BF16)] * part.size, [own, arrived]
        )

    def to_parts(cuts):
        return [cuts[0]] + [part.shifted(cuts[k], k) for k in range(1, part.size)]

    def slots(position, size, count):
        for k in range(size):
            slot = (position - k + size) % size
            yield k, pl.ds(pl.multiple_of(slot * count, count), count)

    def order_rows(pieces):
        def body(ins, outs, _):
            for k, rows in slots(lax.axis_index("mp") // core.size, part.size, half_rows):
                outs[0][rows, :] = ins[k][...]

        return order.ride(body, [struct((half_rows * part.size, part_cols), BF16)], pieces)

    def widened(rows):
        return [rows] + wide.from_others(rows)

    def pack(has_features, width_count):
        return struct((m, (own_cols if has_features else 0) + width_count * half_width), BF16)

    class Gather:
        def __init__(self, keep, sends, has_features, width_count):
            self.base = own_cols if has_features else 0
            self.width_count = width_count
            self.parts = [keep] + [core.shifted(sends[k - 1], k) for k in range(1, core.size)]

        def join(self):
            count = band.size if self.width_count else 1
            base = self.base

            def body(ins, outs, _):
                for c, ref in enumerate(ins):
                    rows = slice(c * m, (c + 1) * m)
                    for k in range(count):
                        if base:
                            outs[k][rows, :base] = ref[:, :base]
                        for index in range(self.width_count):
                            first = base + index * half_width + (-k) % band.size * own_rows
                            target = base + index * own_rows
                            outs[k][rows, target : target + own_rows] = ref[
                                :, first : first + own_rows
                            ]

            cols = base + self.width_count * own_rows
            self.joining = order.ride(
                body, [struct((m * core.size, cols), BF16)] * count, self.parts
            )

        def join_for_role(self):
            self.join()

            def body(ins, outs, _):
                for c, ref in enumerate(ins):
                    outs[0][c * m : (c + 1) * m, :] = ref[...]

            cols = self.base + self.width_count * half_width
            self.whole = order.ride(body, [struct((m * core.size, cols), BF16)], self.parts)

        def send_role_first(self):
            (whole,) = self.whole.results
            cuts = self.joining.results
            self.kept = cuts[0]
            self.banded = merged(
                [band.shifted(cuts[k % len(cuts)], k) for k in range(1, band.size)]
            )
            self.crossed = role.from_others(whole)

        def cut_crossed(self):
            base = self.base

            def body(ins, outs, _):
                for number, ref in enumerate(ins):
                    for k in range(band.size):
                        out = outs[number * band.size + k]
                        out[:, :base] = ref[:, :base]
                        for index in range(self.width_count):
                            first = base + index * half_width + (-k) % band.size * own_rows
                            target = base + index * own_rows
                            out[:, target : target + own_rows] = ref[:, first : first + own_rows]

            cols = base + self.width_count * own_rows
            self.cutting = order.ride(
                body,
                [struct((m * core.size, cols), BF16)] * (band.size * len(self.crossed)),
                self.crossed,
            )

        def band_crossed(self):
            self.arrived = []
            cuts = self.cutting.results
            for number in range(len(self.crossed)):
                own = cuts[number * band.size : (number + 1) * band.size]
                self.arrived += [own[0]] + merged(
                    [band.shifted(own[k], k) for k in range(1, band.size)]
                )

        def send(self):
            cuts = self.joining.results
            self.kept = cuts[0]
            self.banded = merged(
                [band.shifted(cuts[k % len(cuts)], k) for k in range(1, band.size)]
            )
            self.arrived = role.from_others(self.kept)

        def relay(self):
            self.relaying = relayed(self.banded)

        def forward(self, relayed_too=True):
            self.banded = self.relaying.results if relayed_too else self.banded
            for piece in self.banded:
                self.arrived = self.arrived + role.from_others(piece)

        def pieces(self):
            return [self.kept] + self.banded + self.arrived

    def product(lefts, left_col, rights, right_col):
        left = [ref[:, left_col : left_col + own_rows] for ref in lefts]
        right = [ref[:, right_col : right_col + own_cols] for ref in rights]
        return cols_dot(jnp.concatenate(left, axis=0), jnp.concatenate(right, axis=0))

    def begun_gradient(lefts, left_col, rights, right_col):
        count = len(lefts)

        def body(ins, outs, _):
            outs[0][...] = product(ins[:count], left_col, ins[count:], right_col)

        return order.ride(body, [struct((own_rows, own_cols), F32)], lefts + rights)

    def selected_state(own, arrived):
        def body(ins, outs, scratch):
            solving = lax.axis_index("role") == SOLVER
            (sem,) = scratch
            for chosen, source in ((solving, ins[0]), (jnp.logical_not(solving), ins[1])):

                @pl.when(chosen)
                def _():
                    copy = pltpu.make_async_copy(source, outs[0], sem)
                    copy.start()
                    copy.wait()

        scratch = [pltpu.SemaphoreType.DMA]
        outs = [struct(own.shape, F32)]
        return order.call(body, "state", outs, [own, arrived], in_hbm=(0,), scratch=scratch)[0]

    m = half_rows * part.size * wide.size
    total_rows = m * core.size * band.size * role.size
    loss_scale = float(total_rows) ** (-0.5)

    arrived_embed = lax.ppermute(embed[0], "role", to_solver)
    edge_struct = struct(cells.shape[:2] + (STEPS, cells.shape[3]), F32)
    *start_halves, first_rows, last_rows, cells = order.call(
        patches_of,
        "patches",
        [struct((half_rows, features), BF16)] * 2 + [edge_struct] * 2 + [struct(cells.shape, F32)],
        [cells],
    )
    arrived_start = lax.ppermute(start_halves[1], "role", to_trainer)
    head_rows = lax.ppermute(last_rows, "dp", around("dp", 1))
    tail_rows = lax.ppermute(first_rows, "dp", around("dp", -1))
    splitting = split_patches(start_halves[0], arrived_start)
    order.wait_for([head_rows, tail_rows])
    order.run("split")
    embed_kept, up_block = keep_arrived(arrived_embed, embed, 0, mlp, (0, 0))
    embed_own, embed_bands = own_pieces(embed_kept)
    arrived_up = lax.ppermute(up_block, "role", to_solver)
    ordering = order_rows(to_parts(splitting.results))
    edging = packed_edges(order, cells, head_rows, tail_rows, STEPS)
    order.run("order")
    input_parts = widened(*ordering.results)
    (edges,) = edging.results
    from_left = lax.ppermute(edges, "mp", around("mp", 1))
    from_right = lax.ppermute(edges, "mp", around("mp", -1))
    up_kept, down_block = keep_arrived(arrived_up, mlp, (0, 0), mlp, (0, 1))
    up_own, up_bands = own_pieces(up_kept)
    arrived_down = lax.ppermute(down_block, "role", to_solver)
    relay = relayed(merged(embed_bands))
    order.wait_for([from_left, from_right] + input_parts[1:])
    order.run("relay")
    embed_held = held_matrix(embed_own, relay)

    def embed_rows(ins, outs, _):
        parts, matrix = ins[: wide.size], ins[wide.size :]
        *inputs, mine, sent = outs
        position = lax.axis_index("dp") // band.size
        for k, rows in slots(position, wide.size, half_rows * part.size):
            for t in range(core.size):
                inputs[t][rows, :] = parts[k][:, t * own_cols : (t + 1) * own_cols]
        value = embed_held.to_width(matrix, jnp.concatenate([ref[...] for ref in inputs], axis=1))
        mine[...] = value
        sent[...] = value.astype(BF16)

    *inputs, embed_mine, embed_sum = order.call(
        embed_rows,
        "embed",
        [struct((m, own_cols), BF16)] * core.size
        + [struct((m, half_width), F32), struct((m, half_width), BF16)],
        input_parts + embed_held.flat,
    )
    embed_others = part.from_others(embed_sum)

    def core_slot(k):
        return slice((-k) % core.size * own_cols, ((-k) % core.size + 1) * own_cols)

    final_cells, *end_halves = stepped(
        order, cells, head_rows, tail_rows, from_left, from_right, STEPS, 2
    )
    (arrived_end,) = role.from_others(end_halves[1])
    relay = relayed(merged(up_bands))
    order.wait_for(embed_others)
    (down_kept,) = keep_arrived(arrived_down, mlp, (0, 1), None, ())
    down_own, down_bands = own_pieces(down_kept)
    up_held = held_matrix(up_own, relay)
    copying = relayed([final_cells])

    def added(mine, refs, cols):
        total = mine[...]
        for ref in refs:
            total = total + ref[:, :cols].astype(F32)
        return total

    def up_rows(ins, outs, _):
        others, matrix = ins[1 : part.size], ins[part.size :]
        embedded, mine, sent = outs
        value = added(ins[0], others, half_width)
        embedded[...] = value
        hidden = up_held.to_cols(matrix, value.astype(BF16))
        mine[...] = hidden
        sent[...] = with_scalars(hidden, jnp.sum(value * value, axis=1, keepdims=True))

    embedded, up_mine, up_sum = order.call(
        up_rows,
        "up",
        [
            struct((m, half_width), F32),
            struct((m, part_cols), F32),
            struct((m, part_cols + LANES), BF16),
        ],
        [embed_mine] + embed_others + up_held.flat,
    )
    up_others = wide.from_others(up_sum)
    (arrived_cells,) = role.from_others(copying.results[0])
    order.wait_for(up_others + [arrived_cells])
    splitting = split_patches(end_halves[0], arrived_end)
    inputs_on = Gather(inputs[0], [inputs[(-k) % core.size] for k in range(1, core.size)], True, 0)
    inputs_on.join()
    relay = relayed(merged(down_bands))
    order.run("relay")
    down_held = held_matrix(down_own, relay)
    target_cuts = to_parts(splitting.results)
    inputs_on.send()

    def down_rows(ins, outs, _):
        value, others, matrix = ins[0][...], ins[2 : 1 + wide.size], ins[1 + wide.size :]
        hidden, mine, sent, scale, *packs = outs
        squares = jnp.sum(value * value, axis=1, keepdims=True)
        for ref in others:
            squares = squares + scalars_of(ref)
        recip = lax.rsqrt(squares / width + 1e-06)
        preact = added(ins[1], others, part_cols) * recip
        hidden[...] = preact
        normed = (value * recip).astype(BF16)
        _, tangent = gelu_parts(preact)
        active = (0.5 * preact * (1.0 + tangent)).astype(BF16)
        branch = down_held.to_width(matrix, active)
        mine[...] = branch
        sent[...] = branch.astype(BF16)
        scale[...] = jnp.broadcast_to(recip, scale.shape)
        for k in range(core.size):
            packs[k][:, :own_cols] = active[:, core_slot(k)]
            packs[k][:, own_cols:] = normed

    hidden_pre, down_mine, down_sum, scale, *active_packs = order.call(
        down_rows,
        "down",
        [
            struct((m, part_cols), F32),
            struct((m, half_width), F32),
            struct((m, half_width), BF16),
            struct((m, LANES), F32),
        ]
        + [pack(True, 1)] * core.size,
        [embedded, up_mine] + up_others + down_held.flat,
    )
    down_others = part.from_others(down_sum)
    active_on = Gather(active_packs[0], active_packs[1:], True, 1)
    active_on.join()
    inputs_on.relay()
    order.wait_for(inputs_on.arrived)

    def predict_rows(ins, outs, _):
        aims, ins = ins[: part.size], ins[part.size :]
        others, matrix = ins[2 : 1 + part.size], ins[1 + part.size :]
        mine, sent, stream = outs
        value = (ins[0][...] + added(ins[1], others, half_width)).astype(BF16)
        stream[...] = value
        mine[...] = embed_held.to_cols(matrix, value)
        position = lax.axis_index("dp") // band.size * part.size
        for k, ref in enumerate(aims):
            slot = (lax.axis_index("mp") // core.size - k + part.size) % part.size
            rows = pl.ds(pl.multiple_of((position + slot) * half_rows, half_rows), half_rows)
            mine[rows, :] = mine[rows, :] - ref[...].astype(F32)
        sent[...] = mine[...].astype(BF16)

    predict_mine, predict_sum, stream = order.call(
        predict_rows,
        "predict",
        [
            struct((m, part_cols), F32),
            struct((m, part_cols), BF16),
            struct((m, half_width), BF16),
        ],
        target_cuts + [embedded, down_mine] + down_others + embed_held.flat,
    )
    predict_others = wide.from_others(predict_sum)
    inputs_on.forward()
    active_on.send()
    active_on.relay()
    order.wait_for(inputs_on.arrived + active_on.arrived)

    def residual_rows(ins, outs, _):
        inputs, ins = ins[: core.size], ins[core.size :]
        mine_in, others, ins = ins[0], ins[1 : wide.size], ins[wide.size :]
        stream, matrix = ins[0], ins[1:]
        mine, sent, *packs = outs
        known = jnp.concatenate([ref[...] for ref in inputs], axis=1).astype(F32)
        value = ((known + added(mine_in, others, part_cols)) * loss_scale).astype(BF16)
        for k in range(core.size):
            packs[k][:, :own_cols] = value[:, core_slot(k)]
            packs[k][:, own_cols:] = stream[...]
        grad = embed_held.to_width(matrix, value)
        mine[...] = grad
        sent[...] = grad.astype(BF16)

    stream_mine, stream_sum, *residual_packs = order.call(
        residual_rows,
        "residual",
        [struct((m, half_width), F32), struct((m, half_width), BF16)]
        + [pack(True, 1)] * core.size,
        inputs + [predict_mine] + predict_others + [stream] + embed_held.flat,
    )
    stream_others = part.from_others(stream_sum)

    active_on.forward()
    residual_on = Gather(residual_packs[0], residual_packs[1:], True, 1)
    residual_on.join_for_role()

    def hidden_rows(ins, outs, _):
        others, matrix = ins[1 : part.size], ins[part.size :]
        grad, mine, sent, rounded_out = outs
        value = added(ins[0], others, half_width)
        grad[...] = value
        rounded = value.astype(BF16)
        back = down_held.to_cols(matrix, rounded)
        mine[...] = back
        sent[...] = back.astype(BF16)
        rounded_out[...] = rounded

    stream_grad, back_mine, back_sum, stream_sent = order.call(
        hidden_rows,
        "hidden",
        [
            struct((m, half_width), F32),
            struct((m, part_cols), F32),
            struct((m, part_cols), BF16),
            struct((m, half_width), BF16),
        ],
        [stream_mine] + stream_others + down_held.flat,
    )
    back_others = wide.from_others(back_sum)
    residual_on.send_role_first()
    order.wait_for(active_on.arrived + residual_on.banded + residual_on.crossed)

    def normed_rows(ins, outs, _):
        stream_sent, others, matrix = ins[2], ins[3 : 2 + wide.size], ins[2 + wide.size :]
        mine, inner, sent, *packs = outs
        preact = ins[0][...]
        squared, tangent = gelu_parts(preact)
        slope = 0.5 * (1.0 + tangent) + 0.5 * preact * (1.0 - tangent * tangent) * GELU_FACTOR * (
            1.0 + 3.0 * 0.044715 * squared
        )
        value = (added(ins[1], others, part_cols) * slope).astype(BF16)
        for k in range(core.size):
            packs[k][:, :own_cols] = value[:, core_slot(k)]
            packs[k][:, own_cols:] = stream_sent[...]
        grad = up_held.to_width(matrix, value)
        mine[...] = grad
        both = jnp.sum(value.astype(F32) * preact, axis=1, keepdims=True)
        inner[...] = jnp.broadcast_to(both, inner.shape)
        sent[...] = with_scalars(grad, both)

    normed_mine, inner_mine, normed_sum, *hidden_packs = order.call(
        normed_rows,
        "normed",
        [
            struct((m, half_width), F32),
            struct((m, LANES), F32),
            struct((m, half_width + LANES), BF16),
        ]
        + [pack(True, 1)] * core.size,
        [hidden_pre, back_mine, stream_sent] + back_others + up_held.flat,
    )
    normed_others = part.from_others(normed_sum)
    hidden_on = Gather(hidden_packs[0], hidden_packs[1:], True, 1)
    hidden_on.join()
    order.run("join")
    hidden_on.send()
    order.wait_for(hidden_on.arrived)
    hidden_on.forward(False)
    residual_on.cut_crossed()

    def embed_grad_rows(ins, outs, _):
        value, grad, scale_ref, mine, inner_ref, *others = ins
        normed_grad = added(mine, others, half_width)
        inner = inner_ref[:, :1]
        for ref in others:
            inner = inner + scalars_of(ref)
        recip = scale_ref[:, :1]
        outs[0][...] = (
            grad[...] + recip * normed_grad - value[...] * (recip * recip) * (inner / width)
        ).astype(BF16)

    (embed_sent,) = order.call(
        embed_grad_rows,
        "embed_grad",
        [pack(False, 1)],
        [embedded, stream_grad, scale, normed_mine, inner_mine] + normed_others,
    )
    embed_sent_on = Gather(embed_sent, [embed_sent] * (core.size - 1), False, 1)
    embed_sent_on.join()
    order.run("join")
    embed_sent_on.send()
    embed_sent_on.forward(False)
    residual_on.band_crossed()
    all_residual = residual_on.pieces()
    embed_term = begun_gradient(all_residual, own_cols, all_residual, 0)
    state_out = selected_state(final_cells, arrived_cells)

    def updated(name, products, momentum, weight, term=()):
        arrays = [v for _, lefts, _, rights, _ in products for v in lefts + rights] + list(term)
        cuts = 2
        step = own_rows // cuts
        blocks = len(products)

        def body(ins, outs, scratch):
            mom_new, weight_new, sems = scratch
            mom, old = ins[len(arrays)], ins[len(arrays) + 1]
            copies, first = [], 0
            for block, (index, lefts, left_col, rights, right_col) in enumerate(products):
                middle, last = first + len(lefts), first + len(lefts) + len(rights)
                total = product(ins[first:middle], left_col, ins[middle:last], right_col)
                first = last
                for ref in ins[first : first + len(term)]:
                    total = total + ref[...]
                for cut in range(cuts):
                    rows = slice(cut * step, (cut + 1) * step)
                    fresh = MOMENTUM_DECAY * mom[index][rows] + total[rows]
                    mom_new[block, rows, :] = fresh
                    weight_new[block, rows, :] = (
                        old[index][rows].astype(F32) - LEARNING_RATE * fresh
                    ).astype(BF16)
                    for number, source in enumerate((mom_new, weight_new)):
                        copies.append(
                            pltpu.make_async_copy(
                                source.at[block, pl.ds(cut * step, step)],
                                outs[number].at[index].at[pl.ds(cut * step, step)],
                                sems.at[(block * cuts + cut) * 2 + number],
                            )
                        )
                        copies[-1].start()
            for copy in copies:
                copy.wait()

        return order.call(
            body,
            name,
            [struct(momentum.shape, F32), struct(weight.shape, BF16)],
            arrays + [momentum, weight],
            in_hbm=(0, 1),
            scratch=[
                pltpu.VMEM((blocks, own_rows, own_cols), F32),
                pltpu.VMEM((blocks, own_rows, own_cols), BF16),
                pltpu.SemaphoreType.DMA((2 * cuts * blocks,)),
            ],
        )

    all_inputs, all_active = inputs_on.pieces(), active_on.pieces()
    all_hidden, all_embed_sent = hidden_on.pieces(), embed_sent_on.pieces()
    mom_mlp_out, mlp_out = updated(
        "update_mlp",
        [
            ((0, 0), all_active, own_cols, all_hidden, 0),
            ((0, 1), all_hidden, own_cols, all_active, 0),
        ],
        mom_mlp,
        mlp,
    )
    mom_embed_out, embed_out = updated(
        "update_embed",
        [(0, all_embed_sent, 0, all_inputs, 0)],
        mom_embed,
        embed,
        embed_term.results,
    )
    return (state_out, embed_out, mlp_out, mom_embed_out, mom_mlp_out)


def solution(mesh):
    placed = (
        P("role", None, None, "dp", "mp"),
        P("role", "dp", "mp"),
        P("role", None, "dp", "mp"),
        P("role", "dp", "mp"),
        P("role", None, "dp", "mp"),
    )
    return jax.shard_map(
        shards,
        mesh=mesh,
        in_specs=placed,
        out_specs=(
            P(None, None, "dp", "mp"),
            P("role", "dp", "mp"),
            P("role", None, "dp", "mp"),
            P("role", "dp", "mp"),
            P("role", None, "dp", "mp"),
        ),
        check_vma=False,
    )
```

```python
import jax
import jax.numpy as jnp
from jax import lax
from jax.experimental import pallas as pl
from jax.experimental.pallas import tpu as pltpu
from jax.sharding import PartitionSpec as P

PATCH = 16
STEPS = 4


SUBSTRATE_DIFFUSION = 0.2
CATALYST_DIFFUSION = 0.1
FEED_RATE = 0.037
KILL_RATE = 0.06
TIME_STEP = 0.8
GELU_FACTOR = 0.7978845608028654
MOMENTUM_DECAY = 0.9
LEARNING_RATE = 0.003

SOLVER, TRAINER = 0, 1
BF16 = jnp.bfloat16
F32 = jnp.float32


class Digit:
    def __init__(self, axis, stride, size):
        self.axis, self.stride, self.size = axis, stride, size

    def shifted(self, value, step):
        pairs = []
        for index in range(lax.axis_size(self.axis)):
            digit = index // self.stride % self.size
            pairs.append((index, index + ((digit + step) % self.size - digit) * self.stride))
        return lax.ppermute(value, self.axis, pairs)

    def from_others(self, value):
        return [self.shifted(value, k) for k in range(1, self.size)]


def rows_dot(left, right):
    return lax.dot_general(left, right, (((1,), (1,)), ((), ())), preferred_element_type=F32)


def cols_dot(left, right):
    return lax.dot_general(left, right, (((0,), (0,)), ((), ())), preferred_element_type=F32)


def dot(left, right):
    return jnp.dot(left, right, preferred_element_type=F32)


def struct(shape, dtype):
    return jax.ShapeDtypeStruct(shape, dtype)


TOKEN = (8, 128)
CHEAP = pl.CostEstimate(flops=1, transcendentals=0, bytes_accessed=1)


class Work:
    def __init__(self, body, outs, args, in_hbm=(), scratch=(), aliases=None, extra=(), left=()):
        self.body, self.outs, self.args = body, list(outs), list(args)
        self.in_hbm, self.scratch, self.aliases = in_hbm, list(scratch), aliases or {}
        self.extra, self.left, self.results = list(extra), left, None


class Order:
    def __init__(self):
        self.token, self.pending, self.riders = None, [], []

    def wait_for(self, arrays):
        self.pending = self.pending + list(arrays)

    def ride(self, *args, **kwargs):
        self.riders.append(Work(*args, **kwargs))
        return self.riders[-1]

    def run(self, name):
        last = self.riders.pop()
        last.results = self.call(
            last.body,
            name,
            last.outs,
            last.args,
            in_hbm=last.in_hbm,
            scratch=last.scratch,
            left=last.left,
        )

    def call(self, body, name, outs, args, **kwargs):
        works = self.riders + [Work(body, outs, args, **kwargs)]
        after = ([] if self.token is None else [self.token]) + self.pending
        self.pending, self.riders = [], []
        vmem, anywhere = pl.BlockSpec(memory_space=pltpu.VMEM), pl.BlockSpec(memory_space=pl.ANY)
        hbm = pl.BlockSpec(memory_space=pltpu.HBM)
        args, in_specs, outs, out_specs, scratch, aliases, room = [], [], [], [], [], {}, 0
        spans = []
        for work in works:
            spans.append((len(args), len(outs), len(scratch)))
            for index, target in work.aliases.items():
                aliases[len(args) + index] = len(outs) + target
            for k, value in enumerate(work.args):
                in_specs.append(hbm if k in work.left else vmem)
                if k in work.left:
                    work.args[k] = pltpu.with_memory_space_constraint(value, pltpu.HBM)
                room += 0 if k in work.left else value.size * value.dtype.itemsize
            for k, value in enumerate(work.outs):
                out_specs.append(hbm if k in work.in_hbm else vmem)
                room += 0 if k in work.in_hbm else value.size * value.dtype.itemsize
            in_specs += [hbm] * len(work.extra)
            args += work.args + work.extra
            outs += work.outs
            scratch += work.scratch
        in_count, out_count = len(args) + len(after), len(outs) + 1

        def kernel(*refs):
            ins, outs_refs, scratch_refs = (
                refs[:in_count],
                refs[in_count : in_count + out_count],
                refs[in_count + out_count :],
            )
            outs_refs[-1][...] = jnp.zeros(TOKEN, F32)
            for work, (first, out, extra) in zip(works, spans):
                work.body(
                    ins[first : first + len(work.args)],
                    outs_refs[out : out + len(work.outs)],
                    scratch_refs[extra : extra + len(work.scratch)],
                )

        *results, self.token = pl.pallas_call(
            kernel,
            name=name,
            out_shape=outs + [struct(TOKEN, F32)],
            in_specs=in_specs + [anywhere] * len(after),
            out_specs=out_specs + [vmem],
            scratch_shapes=scratch,
            input_output_aliases=aliases,
            compiler_params=pltpu.CompilerParams(
                vmem_limit_bytes=min(56 * 2**20, room + 12 * 2**20)
            ),
            cost_estimate=CHEAP,
        )(*args, *after)
        for work, (_, out, _) in zip(works, spans):
            work.results = results[out : out + len(work.outs)]
        return works[-1].results


class Matrix:
    def __init__(self, pieces):
        self.pieces = pieces
        self.row_count, self.col_count = len(pieces), len(pieces[0])
        self.flat = [piece for row in pieces for piece in row]
        self.rows = sum(row[0].shape[0] for row in pieces)
        self.cols = sum(piece.shape[1] for piece in pieces[0])

    def grid(self, refs):
        return [
            refs[index * self.col_count : (index + 1) * self.col_count]
            for index in range(self.row_count)
        ]

    def to_width(self, refs, value):
        done = []
        for row in self.grid(refs):
            total, first = None, 0
            for ref in row:
                term = rows_dot(value[:, first : first + ref.shape[1]], ref[...])
                total = term if total is None else total + term
                first += ref.shape[1]
            done.append(total)
        return jnp.concatenate(done, axis=1) if len(done) > 1 else done[0]

    def to_cols(self, refs, value):
        done = []
        for col in range(self.col_count):
            total, first = None, 0
            for row in self.grid(refs):
                ref = row[col]
                term = dot(value[:, first : first + ref.shape[0]], ref[...])
                total = term if total is None else total + term
                first += ref.shape[0]
            done.append(total)
        return jnp.concatenate(done, axis=1) if len(done) > 1 else done[0]


LANES = 128


def with_scalars(value, column):
    high = column.astype(BF16).astype(F32)
    low = column - high
    lane = lax.broadcasted_iota(jnp.int32, (value.shape[0], LANES), 1)
    extra = jnp.where(lane == 0, high, jnp.where(lane == 1, low, 0.0))
    return jnp.concatenate([value.astype(BF16), extra.astype(BF16)], axis=1)


def scalars_of(received):
    extra = received[:, received.shape[1] - LANES :].astype(F32)
    return jnp.sum(extra, axis=1, keepdims=True)


def swapped_tiles(cells):
    count = cells.shape[0]
    row = lax.broadcasted_iota(jnp.int32, cells.shape, 0)
    run = lax.broadcasted_iota(jnp.int32, cells.shape, 1) // PATCH
    for bit in (1, 2, 4):
        row_set, run_set = (row & bit) != 0, (run & bit) != 0
        moved = jnp.where(
            row_set, pltpu.roll(cells, bit, 0), pltpu.roll(cells, count - bit, 0)
        )
        shift = bit * PATCH
        moved = jnp.where(
            run_set, pltpu.roll(moved, shift, 1), pltpu.roll(moved, LANES - shift, 1)
        )
        cells = jnp.where(row_set == run_set, cells, moved)
    return cells


def write_patches(tile, outs):
    bands = len(outs)
    species, planes = tile.counts
    for s in range(species):
        for p in range(planes):
            plane = swapped_tiles(tile(s, p))
            octets = PATCH // 8
            groups = plane.shape[0] // PATCH
            each = groups // bands
            for o in range(octets):
                col = ((s * planes + p) * octets + o) * LANES
                for index, out in enumerate(outs):
                    rows = [
                        plane[(g * octets + o) * 8 : (g * octets + o + 1) * 8]
                        for g in range(index * each, (index + 1) * each)
                    ]
                    out[:, col : col + LANES] = jnp.concatenate(rows, axis=0).astype(BF16)


class Tile:
    def __init__(self, read, counts):
        self.read, self.counts = read, counts

    def __call__(self, s, p):
        return self.read(s, p)


def packed_edges(order, cells, head_rows, tail_rows, width):
    species, planes, rows, _ = cells.shape
    tall = rows + 2 * width

    def body(ins, outs, _):
        middle, head, tail = ins
        lane = lax.broadcasted_iota(jnp.int32, (tall, LANES), 1)
        total = jnp.zeros((tall, LANES), F32)
        for s in range(species):
            for p in range(planes):
                plane = jnp.concatenate([head[s, p], middle[s, p], tail[s, p]], axis=0)
                slot = (s * planes + p) * width
                first = plane if slot == 0 else pltpu.roll(plane, slot, 1)
                last = pltpu.roll(plane, (LANES // 2 + slot + width) % LANES, 1)
                total = jnp.where((lane >= slot) & (lane < slot + width), first, total)
                start = LANES // 2 + slot
                total = jnp.where((lane >= start) & (lane < start + width), last, total)
        outs[0][...] = total

    return order.ride(body, [struct((tall, LANES), F32)], [cells, head_rows, tail_rows])


def stepped(order, cells, head_rows, tail_rows, from_left, from_right, width, halves):
    species, planes, rows, cols = cells.shape
    tall = rows + 2 * width
    patch_rows = rows // PATCH * (cols // PATCH) // halves
    features = species * planes * PATCH * PATCH

    def body(ins, outs, scratch):
        middle, head, tail, left, right = ins
        (final, *patches), (now, later) = outs, scratch
        lane = lax.broadcasted_iota(jnp.int32, (tall, LANES), 1)
        from_l, from_r = left[...], right[...]
        for s in range(species):
            for p in range(planes):
                slot = (s * planes + p) * width
                now[0, s, p] = jnp.concatenate([head[s, p], middle[s, p], tail[s, p]], axis=0)
                ahead = from_r if slot == 0 else pltpu.roll(from_r, LANES - slot, 1)
                behind = pltpu.roll(from_l, LANES // 2 - slot - width, 1)
                halo = jnp.where(lane < width, ahead, 0.0)
                now[1, s, p] = jnp.where(lane >= LANES - width, behind, halo)

        def neighbours(field, halo):
            up_f, down_f = pltpu.roll(field, 1, 0), pltpu.roll(field, tall - 1, 0)
            up_h, down_h = pltpu.roll(halo, 1, 0), pltpu.roll(halo, tall - 1, 0)
            before_f, before_h = pltpu.roll(field, 1, 1), pltpu.roll(halo, 1, 1)
            after_f, after_h = pltpu.roll(field, LANES - 1, 1), pltpu.roll(halo, LANES - 1, 1)
            first, last = lane == 0, lane == LANES - 1
            sum_f = up_f + down_f + jnp.where(first, before_h, before_f)
            sum_f = sum_f + jnp.where(last, after_h, after_f)
            sum_h = up_h + down_h + jnp.where(first, before_f, before_h)
            sum_h = sum_h + jnp.where(last, after_f, after_h)
            return sum_f, sum_h

        for step in range(STEPS):
            source, target = (now, later) if step % 2 == 0 else (later, now)

            def one_plane(p, carry):
                below, above = jnp.maximum(p - 1, 0), jnp.minimum(p + 1, planes - 1)
                beside = [neighbours(source[0, s, p], source[1, s, p]) for s in range(2)]
                for layer in range(2):
                    u, v = source[layer, 0, p], source[layer, 1, p]
                    lap = []
                    for s, centre in ((0, u), (1, v)):
                        total = source[layer, s, below] + source[layer, s, above]
                        lap.append(total + beside[s][layer] - 6.0 * centre)
                    growth = u * v * v
                    target[layer, 0, p] = u + TIME_STEP * (
                        SUBSTRATE_DIFFUSION * lap[0] - growth + FEED_RATE * (1.0 - u)
                    )
                    target[layer, 1, p] = v + TIME_STEP * (
                        CATALYST_DIFFUSION * lap[1] + growth - (FEED_RATE + KILL_RATE) * v
                    )
                return carry

            lax.fori_loop(0, planes, one_plane, 0)
        source = now if STEPS % 2 == 0 else later
        for s in range(species):
            for p in range(planes):
                final[s, p] = source[0, s, p, width : width + rows]
        write_patches(Tile(lambda s, p: final[s, p], (species, planes)), patches)

    return order.call(
        body,
        "stencil",
        [struct(cells.shape, F32)] + [struct((patch_rows, features), BF16)] * halves,
        [cells, head_rows, tail_rows, from_left, from_right],
        scratch=[pltpu.VMEM((2, species, planes, tall, LANES), F32)] * 2,
    )


def gelu_parts(preact):
    squared = preact * preact
    tangent = jnp.tanh(GELU_FACTOR * (preact + 0.044715 * preact * squared))
    return squared, tangent


def shards(state, embed, mlp, mom_embed, mom_mlp):
    dp_count, mp_count = lax.axis_size("dp"), lax.axis_size("mp")
    halves = 2 if dp_count % 2 == 0 else 1
    pairs = 2 if mp_count % 2 == 0 else 1
    wide = Digit("dp", dp_count // halves, halves)
    band = Digit("dp", 1, dp_count // halves)
    part = Digit("mp", pairs, mp_count // pairs)
    core = Digit("mp", 1, pairs)
    role = Digit("role", 1, lax.axis_size("role"))
    width = embed.shape[1] * dp_count
    own_rows, own_cols = embed.shape[1], embed.shape[2]
    half_width, part_cols = own_rows * band.size, own_cols * core.size
    to_solver, to_trainer = [(TRAINER, SOLVER)], [(SOLVER, TRAINER)]
    order = Order()

    def keep_arrived(arrived, own, index, following):
        def body(ins, outs, scratch):
            (sems,) = scratch
            solving = lax.axis_index("role") == SOLVER
            ahead = [
                pltpu.make_async_copy(ins[2].at[block], outs[1 + k], sems.at[1 + k])
                for k, block in enumerate(following)
            ]
            for copy in ahead:
                copy.start()

            @pl.when(solving)
            def _():
                outs[0][...] = ins[0][...]

            @pl.when(jnp.logical_not(solving))
            def _():
                mine = pltpu.make_async_copy(ins[1].at[index], outs[0], sems.at[0])
                mine.start()
                mine.wait()

            for copy in ahead:
                copy.wait()

        return order.call(
            body,
            "held",
            [struct(arrived.shape, BF16)] * (1 + len(following)),
            [arrived, own] + ([mlp] if following else []),
            left=(1, 2),
            scratch=[pltpu.SemaphoreType.DMA((1 + len(following),))],
        )

    def relayed(blocks):
        def body(ins, outs, _):
            for source, target in zip(ins, outs):
                target[...] = source[...]

        return order.ride(body, [struct(v.shape, v.dtype) for v in blocks], blocks)

    def own_pieces(block):
        return [block] + core.from_others(block), band.from_others(block)

    def merged(parts):
        return [jnp.concatenate(parts, axis=0)] if len(parts) > 1 else parts

    def held_matrix(own, relay):
        return Matrix([own] + [[rows] + core.from_others(rows) for rows in relay.results])

    cells = state[0]
    rows_in = cells.shape[2]
    features = cells.shape[0] * cells.shape[1] * PATCH * PATCH
    half_rows = rows_in // PATCH * (cells.shape[3] // PATCH) // 2

    def around(axis, step):
        count = lax.axis_size(axis)
        return [(i, (i + step) % count) for i in range(count)]

    def patches_of(ins, outs, _):
        counts = (cells.shape[0], cells.shape[1])
        write_patches(Tile(lambda s, p: ins[0][s, p], counts), outs[:2])
        outs[2][...] = ins[0][:, :, :STEPS]
        outs[3][...] = ins[0][:, :, rows_in - STEPS :]
        outs[4][...] = ins[0][...]

    def split_patches(own, arrived):
        def body(ins, outs, _):
            solving = lax.axis_index("role") == SOLVER
            position = lax.axis_index("mp")
            my_part, my_core = position // core.size, position % core.size
            for k in range(part.size):
                for t in range(core.size):
                    quarter = (my_part + k) % part.size * core.size
                    quarter = quarter + (my_core - t + core.size) % core.size
                    source = pl.ds(pl.multiple_of(quarter * own_cols, own_cols), own_cols)
                    cols = slice(t * own_cols, (t + 1) * own_cols)

                    @pl.when(solving)
                    def _():
                        outs[k][:, cols] = ins[0][:, source]

                    @pl.when(jnp.logical_not(solving))
                    def _():
                        outs[k][:, cols] = ins[1][:, source]

        return order.ride(
            body, [struct((half_rows, part_cols), BF16)] * part.size, [own, arrived]
        )

    def to_parts(cuts):
        return [cuts[0]] + [part.shifted(cuts[k], k) for k in range(1, part.size)]

    def slots(position, size, count):
        for k in range(size):
            slot = (position - k + size) % size
            yield k, pl.ds(pl.multiple_of(slot * count, count), count)

    def order_rows(pieces):
        def body(ins, outs, _):
            for k, rows in slots(lax.axis_index("mp") // core.size, part.size, half_rows):
                outs[0][rows, :] = ins[k][...]

        return order.ride(body, [struct((half_rows * part.size, part_cols), BF16)], pieces)

    def widened(rows):
        return [rows] + wide.from_others(rows)

    def pack(has_features, width_count):
        return struct((m, (own_cols if has_features else 0) + width_count * half_width), BF16)

    class Gather:
        def __init__(self, keep, sends, has_features, width_count):
            self.base = own_cols if has_features else 0
            self.width_count = width_count
            self.parts = [keep] + [core.shifted(sends[k - 1], k) for k in range(1, core.size)]

        def join(self):
            count = band.size if self.width_count else 1
            base = self.base

            def body(ins, outs, _):
                for c, ref in enumerate(ins):
                    rows = slice(c * m, (c + 1) * m)
                    for k in range(count):
                        if base:
                            outs[k][rows, :base] = ref[:, :base]
                        for index in range(self.width_count):
                            first = base + index * half_width + (-k) % band.size * own_rows
                            target = base + index * own_rows
                            outs[k][rows, target : target + own_rows] = ref[
                                :, first : first + own_rows
                            ]

            cols = base + self.width_count * own_rows
            self.joining = order.ride(
                body, [struct((m * core.size, cols), BF16)] * count, self.parts
            )

        def join_for_role(self):
            self.join()

            def body(ins, outs, _):
                for c, ref in enumerate(ins):
                    outs[0][c * m : (c + 1) * m, :] = ref[...]

            cols = self.base + self.width_count * half_width
            self.whole = order.ride(body, [struct((m * core.size, cols), BF16)], self.parts)

        def send_role_first(self):
            (whole,) = self.whole.results
            cuts = self.joining.results
            self.kept = cuts[0]
            self.banded = merged(
                [band.shifted(cuts[k % len(cuts)], k) for k in range(1, band.size)]
            )
            self.crossed = role.from_others(whole)

        def cut_crossed(self):
            base = self.base

            def body(ins, outs, _):
                for number, ref in enumerate(ins):
                    for k in range(band.size):
                        out = outs[number * band.size + k]
                        out[:, :base] = ref[:, :base]
                        for index in range(self.width_count):
                            first = base + index * half_width + (-k) % band.size * own_rows
                            target = base + index * own_rows
                            out[:, target : target + own_rows] = ref[:, first : first + own_rows]

            cols = base + self.width_count * own_rows
            self.cutting = order.ride(
                body,
                [struct((m * core.size, cols), BF16)] * (band.size * len(self.crossed)),
                self.crossed,
            )

        def band_crossed(self):
            self.arrived = []
            cuts = self.cutting.results
            for number in range(len(self.crossed)):
                own = cuts[number * band.size : (number + 1) * band.size]
                self.arrived += [own[0]] + merged(
                    [band.shifted(own[k], k) for k in range(1, band.size)]
                )

        def send(self):
            cuts = self.joining.results
            self.kept = cuts[0]
            self.banded = merged(
                [band.shifted(cuts[k % len(cuts)], k) for k in range(1, band.size)]
            )
            self.arrived = role.from_others(self.kept)

        def relay(self):
            self.relaying = relayed(self.banded)

        def forward(self, relayed_too=True):
            self.banded = self.relaying.results if relayed_too else self.banded
            for piece in self.banded:
                self.arrived = self.arrived + role.from_others(piece)

        def pieces(self):
            return [self.kept] + self.banded + self.arrived

    def product(lefts, left_col, rights, right_col):
        left = [ref[:, left_col : left_col + own_rows] for ref in lefts]
        right = [ref[:, right_col : right_col + own_cols] for ref in rights]
        return cols_dot(jnp.concatenate(left, axis=0), jnp.concatenate(right, axis=0))

    def begun_gradient(lefts, left_col, rights, right_col):
        count = len(lefts)

        def body(ins, outs, _):
            outs[0][...] = product(ins[:count], left_col, ins[count:], right_col)

        return order.ride(body, [struct((own_rows, own_cols), F32)], lefts + rights)

    def selected_state(own, arrived):
        def body(ins, outs, scratch):
            solving = lax.axis_index("role") == SOLVER
            (sem,) = scratch
            for chosen, source in ((solving, ins[0]), (jnp.logical_not(solving), ins[1])):

                @pl.when(chosen)
                def _():
                    copy = pltpu.make_async_copy(source, outs[0], sem)
                    copy.start()
                    copy.wait()

        scratch = [pltpu.SemaphoreType.DMA]
        outs = [struct(own.shape, F32)]
        return order.call(body, "state", outs, [own, arrived], in_hbm=(0,), scratch=scratch)[0]

    m = half_rows * part.size * wide.size
    total_rows = m * core.size * band.size * role.size
    loss_scale = float(total_rows) ** (-0.5)

    arrived_embed = lax.ppermute(embed[0], "role", to_solver)
    edge_struct = struct(cells.shape[:2] + (STEPS, cells.shape[3]), F32)
    *start_halves, first_rows, last_rows, cells = order.call(
        patches_of,
        "patches",
        [struct((half_rows, features), BF16)] * 2 + [edge_struct] * 2 + [struct(cells.shape, F32)],
        [cells],
    )
    arrived_start = lax.ppermute(start_halves[1], "role", to_trainer)
    head_rows = lax.ppermute(last_rows, "dp", around("dp", 1))
    tail_rows = lax.ppermute(first_rows, "dp", around("dp", -1))
    splitting = split_patches(start_halves[0], arrived_start)
    order.wait_for([head_rows, tail_rows])
    order.run("split")
    embed_kept, up_block, down_block = keep_arrived(arrived_embed, embed, 0, ((0, 0), (0, 1)))
    embed_own, embed_bands = own_pieces(embed_kept)
    arrived_up = lax.ppermute(up_block, "role", to_solver)
    arrived_down = lax.ppermute(down_block, "role", to_solver)
    ordering = order_rows(to_parts(splitting.results))
    edging = packed_edges(order, cells, head_rows, tail_rows, STEPS)
    order.run("order")
    input_parts = widened(*ordering.results)
    (edges,) = edging.results
    from_left = lax.ppermute(edges, "mp", around("mp", 1))
    from_right = lax.ppermute(edges, "mp", around("mp", -1))
    (up_kept,) = keep_arrived(arrived_up, mlp, (0, 0), ())
    up_own, up_bands = own_pieces(up_kept)
    relay = relayed(merged(embed_bands))
    order.wait_for([from_left, from_right] + input_parts[1:])
    order.run("relay")
    embed_held = held_matrix(embed_own, relay)
    final_cells, *end_halves = stepped(
        order, cells, head_rows, tail_rows, from_left, from_right, STEPS, 2
    )
    (down_kept,) = keep_arrived(arrived_down, mlp, (0, 1), ())
    down_own, down_bands = own_pieces(down_kept)
    up_relay = relayed(merged(up_bands))

    def embed_rows(ins, outs, _):
        parts, matrix = ins[: wide.size], ins[wide.size :]
        *inputs, mine, sent = outs
        position = lax.axis_index("dp") // band.size
        for k, rows in slots(position, wide.size, half_rows * part.size):
            for t in range(core.size):
                inputs[t][rows, :] = parts[k][:, t * own_cols : (t + 1) * own_cols]
        value = embed_held.to_width(matrix, jnp.concatenate([ref[...] for ref in inputs], axis=1))
        mine[...] = value
        sent[...] = value.astype(BF16)

    *inputs, embed_mine, embed_sum = order.call(
        embed_rows,
        "embed",
        [struct((m, own_cols), BF16)] * core.size
        + [struct((m, half_width), F32), struct((m, half_width), BF16)],
        input_parts + embed_held.flat,
    )
    embed_others = part.from_others(embed_sum)

    def core_slot(k):
        return slice((-k) % core.size * own_cols, ((-k) % core.size + 1) * own_cols)

    (arrived_end,) = role.from_others(end_halves[1])
    up_held = held_matrix(up_own, up_relay)
    copying = relayed([final_cells])

    def added(mine, refs, cols):
        total = mine[...]
        for ref in refs:
            total = total + ref[:, :cols].astype(F32)
        return total

    def up_rows(ins, outs, _):
        others, matrix = ins[1 : part.size], ins[part.size :]
        embedded, mine, sent = outs
        value = added(ins[0], others, half_width)
        embedded[...] = value
        hidden = up_held.to_cols(matrix, value.astype(BF16))
        mine[...] = hidden
        sent[...] = with_scalars(hidden, jnp.sum(value * value, axis=1, keepdims=True))

    embedded, up_mine, up_sum = order.call(
        up_rows,
        "up",
        [
            struct((m, half_width), F32),
            struct((m, part_cols), F32),
            struct((m, part_cols + LANES), BF16),
        ],
        [embed_mine] + embed_others + up_held.flat,
    )
    up_others = wide.from_others(up_sum)
    (arrived_cells,) = role.from_others(copying.results[0])
    order.wait_for(up_others + [arrived_cells])
    splitting = split_patches(end_halves[0], arrived_end)
    inputs_on = Gather(inputs[0], [inputs[(-k) % core.size] for k in range(1, core.size)], True, 0)
    inputs_on.join()
    relay = relayed(merged(down_bands))
    order.run("relay")
    down_held = held_matrix(down_own, relay)
    target_cuts = to_parts(splitting.results)
    inputs_on.send()

    def down_rows(ins, outs, _):
        value, others, matrix = ins[0][...], ins[2 : 1 + wide.size], ins[1 + wide.size :]
        hidden, mine, sent, scale, *packs = outs
        squares = jnp.sum(value * value, axis=1, keepdims=True)
        for ref in others:
            squares = squares + scalars_of(ref)
        recip = lax.rsqrt(squares / width + 1e-06)
        preact = added(ins[1], others, part_cols) * recip
        hidden[...] = preact
        normed = (value * recip).astype(BF16)
        _, tangent = gelu_parts(preact)
        active = (0.5 * preact * (1.0 + tangent)).astype(BF16)
        branch = down_held.to_width(matrix, active)
        mine[...] = branch
        sent[...] = branch.astype(BF16)
        scale[...] = jnp.broadcast_to(recip, scale.shape)
        for k in range(core.size):
            packs[k][:, :own_cols] = active[:, core_slot(k)]
            packs[k][:, own_cols:] = normed

    hidden_pre, down_mine, down_sum, scale, *active_packs = order.call(
        down_rows,
        "down",
        [
            struct((m, part_cols), F32),
            struct((m, half_width), F32),
            struct((m, half_width), BF16),
            struct((m, LANES), F32),
        ]
        + [pack(True, 1)] * core.size,
        [embedded, up_mine] + up_others + down_held.flat,
    )
    down_others = part.from_others(down_sum)
    active_on = Gather(active_packs[0], active_packs[1:], True, 1)
    active_on.join()
    inputs_on.relay()
    order.wait_for(inputs_on.arrived)

    def predict_rows(ins, outs, _):
        aims, ins = ins[: part.size], ins[part.size :]
        others, matrix = ins[2 : 1 + part.size], ins[1 + part.size :]
        mine, sent, stream = outs
        value = (ins[0][...] + added(ins[1], others, half_width)).astype(BF16)
        stream[...] = value
        mine[...] = embed_held.to_cols(matrix, value)
        position = lax.axis_index("dp") // band.size * part.size
        for k, ref in enumerate(aims):
            slot = (lax.axis_index("mp") // core.size - k + part.size) % part.size
            rows = pl.ds(pl.multiple_of((position + slot) * half_rows, half_rows), half_rows)
            mine[rows, :] = mine[rows, :] - ref[...].astype(F32)
        sent[...] = mine[...].astype(BF16)

    predict_mine, predict_sum, stream = order.call(
        predict_rows,
        "predict",
        [
            struct((m, part_cols), F32),
            struct((m, part_cols), BF16),
            struct((m, half_width), BF16),
        ],
        target_cuts + [embedded, down_mine] + down_others + embed_held.flat,
    )
    predict_others = wide.from_others(predict_sum)
    inputs_on.forward()
    active_on.send()
    active_on.relay()
    order.wait_for(inputs_on.arrived + active_on.arrived)

    def residual_rows(ins, outs, _):
        inputs, ins = ins[: core.size], ins[core.size :]
        mine_in, others, ins = ins[0], ins[1 : wide.size], ins[wide.size :]
        stream, matrix = ins[0], ins[1:]
        mine, sent, *packs = outs
        known = jnp.concatenate([ref[...] for ref in inputs], axis=1).astype(F32)
        value = ((known + added(mine_in, others, part_cols)) * loss_scale).astype(BF16)
        for k in range(core.size):
            packs[k][:, :own_cols] = value[:, core_slot(k)]
            packs[k][:, own_cols:] = stream[...]
        grad = embed_held.to_width(matrix, value)
        mine[...] = grad
        sent[...] = grad.astype(BF16)

    stream_mine, stream_sum, *residual_packs = order.call(
        residual_rows,
        "residual",
        [struct((m, half_width), F32), struct((m, half_width), BF16)]
        + [pack(True, 1)] * core.size,
        inputs + [predict_mine] + predict_others + [stream] + embed_held.flat,
    )
    stream_others = part.from_others(stream_sum)

    active_on.forward()
    residual_on = Gather(residual_packs[0], residual_packs[1:], True, 1)
    residual_on.join_for_role()

    def hidden_rows(ins, outs, _):
        others, matrix = ins[1 : part.size], ins[part.size :]
        grad, mine, sent, rounded_out = outs
        value = added(ins[0], others, half_width)
        grad[...] = value
        rounded = value.astype(BF16)
        back = down_held.to_cols(matrix, rounded)
        mine[...] = back
        sent[...] = back.astype(BF16)
        rounded_out[...] = rounded

    stream_grad, back_mine, back_sum, stream_sent = order.call(
        hidden_rows,
        "hidden",
        [
            struct((m, half_width), F32),
            struct((m, part_cols), F32),
            struct((m, part_cols), BF16),
            struct((m, half_width), BF16),
        ],
        [stream_mine] + stream_others + down_held.flat,
    )
    back_others = wide.from_others(back_sum)
    residual_on.send_role_first()
    order.wait_for(active_on.arrived + residual_on.banded + residual_on.crossed)

    def normed_rows(ins, outs, _):
        stream_sent, others, matrix = ins[2], ins[3 : 2 + wide.size], ins[2 + wide.size :]
        mine, inner, sent, *packs = outs
        preact = ins[0][...]
        squared, tangent = gelu_parts(preact)
        slope = 0.5 * (1.0 + tangent) + 0.5 * preact * (1.0 - tangent * tangent) * GELU_FACTOR * (
            1.0 + 3.0 * 0.044715 * squared
        )
        value = (added(ins[1], others, part_cols) * slope).astype(BF16)
        for k in range(core.size):
            packs[k][:, :own_cols] = value[:, core_slot(k)]
            packs[k][:, own_cols:] = stream_sent[...]
        grad = up_held.to_width(matrix, value)
        mine[...] = grad
        both = jnp.sum(value.astype(F32) * preact, axis=1, keepdims=True)
        inner[...] = jnp.broadcast_to(both, inner.shape)
        sent[...] = with_scalars(grad, both)

    normed_mine, inner_mine, normed_sum, *hidden_packs = order.call(
        normed_rows,
        "normed",
        [
            struct((m, half_width), F32),
            struct((m, LANES), F32),
            struct((m, half_width + LANES), BF16),
        ]
        + [pack(True, 1)] * core.size,
        [hidden_pre, back_mine, stream_sent] + back_others + up_held.flat,
    )
    normed_others = part.from_others(normed_sum)
    hidden_on = Gather(hidden_packs[0], hidden_packs[1:], True, 1)
    hidden_on.join()
    order.run("join")
    hidden_on.send()
    hidden_kept_arrived = list(hidden_on.arrived)
    hidden_on.forward(False)
    residual_on.cut_crossed()

    def embed_grad_rows(ins, outs, _):
        value, grad, scale_ref, mine, inner_ref, *others = ins
        normed_grad = added(mine, others, half_width)
        inner = inner_ref[:, :1]
        for ref in others:
            inner = inner + scalars_of(ref)
        recip = scale_ref[:, :1]
        outs[0][...] = (
            grad[...] + recip * normed_grad - value[...] * (recip * recip) * (inner / width)
        ).astype(BF16)

    (embed_sent,) = order.call(
        embed_grad_rows,
        "embed_grad",
        [pack(False, 1)],
        [embedded, stream_grad, scale, normed_mine, inner_mine] + normed_others,
    )
    embed_sent_on = Gather(embed_sent, [embed_sent] * (core.size - 1), False, 1)
    embed_sent_on.join()
    order.wait_for(hidden_kept_arrived)
    order.run("join")
    embed_sent_on.send()
    embed_sent_on.forward(False)
    residual_on.band_crossed()
    all_residual = residual_on.pieces()
    embed_term = begun_gradient(all_residual, own_cols, all_residual, 0)
    state_out = selected_state(final_cells, arrived_cells)

    def updated(name, products, momentum, weight, term=()):
        arrays = [v for _, lefts, _, rights, _ in products for v in lefts + rights] + list(term)
        cuts = 2
        step = own_rows // cuts
        blocks = len(products)

        def body(ins, outs, scratch):
            mom_new, weight_new, sems = scratch
            mom, old = ins[len(arrays)], ins[len(arrays) + 1]
            copies, first = [], 0
            for block, (index, lefts, left_col, rights, right_col) in enumerate(products):
                middle, last = first + len(lefts), first + len(lefts) + len(rights)
                total = product(ins[first:middle], left_col, ins[middle:last], right_col)
                first = last
                for ref in ins[first : first + len(term)]:
                    total = total + ref[...]
                for cut in range(cuts):
                    rows = slice(cut * step, (cut + 1) * step)
                    fresh = MOMENTUM_DECAY * mom[index][rows] + total[rows]
                    mom_new[block, rows, :] = fresh
                    weight_new[block, rows, :] = (
                        old[index][rows].astype(F32) - LEARNING_RATE * fresh
                    ).astype(BF16)
                    for number, source in enumerate((mom_new, weight_new)):
                        copies.append(
                            pltpu.make_async_copy(
                                source.at[block, pl.ds(cut * step, step)],
                                outs[number].at[index].at[pl.ds(cut * step, step)],
                                sems.at[(block * cuts + cut) * 2 + number],
                            )
                        )
                        copies[-1].start()
            for copy in copies:
                copy.wait()

        return order.call(
            body,
            name,
            [struct(momentum.shape, F32), struct(weight.shape, BF16)],
            arrays + [momentum, weight],
            in_hbm=(0, 1),
            scratch=[
                pltpu.VMEM((blocks, own_rows, own_cols), F32),
                pltpu.VMEM((blocks, own_rows, own_cols), BF16),
                pltpu.SemaphoreType.DMA((2 * cuts * blocks,)),
            ],
        )

    all_inputs, all_active = inputs_on.pieces(), active_on.pieces()
    all_hidden, all_embed_sent = hidden_on.pieces(), embed_sent_on.pieces()
    mom_mlp_out, mlp_out = updated(
        "update_mlp",
        [
            ((0, 0), all_active, own_cols, all_hidden, 0),
            ((0, 1), all_hidden, own_cols, all_active, 0),
        ],
        mom_mlp,
        mlp,
    )
    mom_embed_out, embed_out = updated(
        "update_embed",
        [(0, all_embed_sent, 0, all_inputs, 0)],
        mom_embed,
        embed,
        embed_term.results,
    )
    return (state_out, embed_out, mlp_out, mom_embed_out, mom_mlp_out)


def solution(mesh):
    placed = (
        P("role", None, None, "dp", "mp"),
        P("role", "dp", "mp"),
        P("role", None, "dp", "mp"),
        P("role", "dp", "mp"),
        P("role", None, "dp", "mp"),
    )
    return jax.shard_map(
        shards,
        mesh=mesh,
        in_specs=placed,
        out_specs=(
            P(None, None, "dp", "mp"),
            P("role", "dp", "mp"),
            P("role", None, "dp", "mp"),
            P("role", "dp", "mp"),
            P("role", None, "dp", "mp"),
        ),
        check_vma=False,
    )
```

```python
import jax
import jax.numpy as jnp
from jax import lax
from jax.experimental import pallas as pl
from jax.experimental.pallas import tpu as pltpu
from jax.sharding import PartitionSpec as P

PATCH = 16
STEPS = 4


SUBSTRATE_DIFFUSION = 0.2
CATALYST_DIFFUSION = 0.1
FEED_RATE = 0.037
KILL_RATE = 0.06
TIME_STEP = 0.8
GELU_FACTOR = 0.7978845608028654
MOMENTUM_DECAY = 0.9
LEARNING_RATE = 0.003

SOLVER, TRAINER = 0, 1
BF16 = jnp.bfloat16
F32 = jnp.float32


class Digit:
    def __init__(self, axis, stride, size):
        self.axis, self.stride, self.size = axis, stride, size

    def shifted(self, value, step):
        pairs = []
        for index in range(lax.axis_size(self.axis)):
            digit = index // self.stride % self.size
            pairs.append((index, index + ((digit + step) % self.size - digit) * self.stride))
        return lax.ppermute(value, self.axis, pairs)

    def from_others(self, value):
        return [self.shifted(value, k) for k in range(1, self.size)]


def rows_dot(left, right):
    return lax.dot_general(left, right, (((1,), (1,)), ((), ())), preferred_element_type=F32)


def cols_dot(left, right):
    return lax.dot_general(left, right, (((0,), (0,)), ((), ())), preferred_element_type=F32)


def dot(left, right):
    return jnp.dot(left, right, preferred_element_type=F32)


def struct(shape, dtype):
    return jax.ShapeDtypeStruct(shape, dtype)


TOKEN = (8, 128)
CHEAP = pl.CostEstimate(flops=1, transcendentals=0, bytes_accessed=1)


class Work:
    def __init__(self, body, outs, args, in_hbm=(), scratch=(), aliases=None, extra=(), left=()):
        self.body, self.outs, self.args = body, list(outs), list(args)
        self.in_hbm, self.scratch, self.aliases = in_hbm, list(scratch), aliases or {}
        self.extra, self.left, self.results = list(extra), left, None


class Order:
    def __init__(self):
        self.token, self.pending, self.riders = None, [], []

    def wait_for(self, arrays):
        self.pending = self.pending + list(arrays)

    def ride(self, *args, **kwargs):
        self.riders.append(Work(*args, **kwargs))
        return self.riders[-1]

    def run(self, name):
        last = self.riders.pop()
        last.results = self.call(
            last.body,
            name,
            last.outs,
            last.args,
            in_hbm=last.in_hbm,
            scratch=last.scratch,
            left=last.left,
        )

    def call(self, body, name, outs, args, **kwargs):
        works = self.riders + [Work(body, outs, args, **kwargs)]
        after = ([] if self.token is None else [self.token]) + self.pending
        self.pending, self.riders = [], []
        vmem, anywhere = pl.BlockSpec(memory_space=pltpu.VMEM), pl.BlockSpec(memory_space=pl.ANY)
        hbm = pl.BlockSpec(memory_space=pltpu.HBM)
        args, in_specs, outs, out_specs, scratch, aliases, room = [], [], [], [], [], {}, 0
        spans = []
        for work in works:
            spans.append((len(args), len(outs), len(scratch)))
            for index, target in work.aliases.items():
                aliases[len(args) + index] = len(outs) + target
            for k, value in enumerate(work.args):
                in_specs.append(hbm if k in work.left else vmem)
                if k in work.left:
                    work.args[k] = pltpu.with_memory_space_constraint(value, pltpu.HBM)
                room += 0 if k in work.left else value.size * value.dtype.itemsize
            for k, value in enumerate(work.outs):
                out_specs.append(hbm if k in work.in_hbm else vmem)
                room += 0 if k in work.in_hbm else value.size * value.dtype.itemsize
            in_specs += [hbm] * len(work.extra)
            args += work.args + work.extra
            outs += work.outs
            scratch += work.scratch
        in_count, out_count = len(args) + len(after), len(outs) + 1

        def kernel(*refs):
            ins, outs_refs, scratch_refs = (
                refs[:in_count],
                refs[in_count : in_count + out_count],
                refs[in_count + out_count :],
            )
            outs_refs[-1][...] = jnp.zeros(TOKEN, F32)
            for work, (first, out, extra) in zip(works, spans):
                work.body(
                    ins[first : first + len(work.args)],
                    outs_refs[out : out + len(work.outs)],
                    scratch_refs[extra : extra + len(work.scratch)],
                )

        *results, self.token = pl.pallas_call(
            kernel,
            name=name,
            out_shape=outs + [struct(TOKEN, F32)],
            in_specs=in_specs + [anywhere] * len(after),
            out_specs=out_specs + [vmem],
            scratch_shapes=scratch,
            input_output_aliases=aliases,
            compiler_params=pltpu.CompilerParams(
                vmem_limit_bytes=min(56 * 2**20, room + 12 * 2**20)
            ),
            cost_estimate=CHEAP,
        )(*args, *after)
        for work, (_, out, _) in zip(works, spans):
            work.results = results[out : out + len(work.outs)]
        return works[-1].results


class Matrix:
    def __init__(self, pieces):
        self.pieces = pieces
        self.row_count, self.col_count = len(pieces), len(pieces[0])
        self.flat = [piece for row in pieces for piece in row]
        self.rows = sum(row[0].shape[0] for row in pieces)
        self.cols = sum(piece.shape[1] for piece in pieces[0])

    def grid(self, refs):
        return [
            refs[index * self.col_count : (index + 1) * self.col_count]
            for index in range(self.row_count)
        ]

    def to_width(self, refs, value):
        done = []
        for row in self.grid(refs):
            total, first = None, 0
            for ref in row:
                term = rows_dot(value[:, first : first + ref.shape[1]], ref[...])
                total = term if total is None else total + term
                first += ref.shape[1]
            done.append(total)
        return jnp.concatenate(done, axis=1) if len(done) > 1 else done[0]

    def to_cols(self, refs, value):
        done = []
        for col in range(self.col_count):
            total, first = None, 0
            for row in self.grid(refs):
                ref = row[col]
                term = dot(value[:, first : first + ref.shape[0]], ref[...])
                total = term if total is None else total + term
                first += ref.shape[0]
            done.append(total)
        return jnp.concatenate(done, axis=1) if len(done) > 1 else done[0]


LANES = 128


def with_scalars(value, column):
    high = column.astype(BF16).astype(F32)
    low = column - high
    lane = lax.broadcasted_iota(jnp.int32, (value.shape[0], LANES), 1)
    extra = jnp.where(lane == 0, high, jnp.where(lane == 1, low, 0.0))
    return jnp.concatenate([value.astype(BF16), extra.astype(BF16)], axis=1)


def scalars_of(received):
    extra = received[:, received.shape[1] - LANES :].astype(F32)
    return jnp.sum(extra, axis=1, keepdims=True)


def swapped_tiles(cells):
    count = cells.shape[0]
    row = lax.broadcasted_iota(jnp.int32, cells.shape, 0)
    run = lax.broadcasted_iota(jnp.int32, cells.shape, 1) // PATCH
    for bit in (1, 2, 4):
        row_set, run_set = (row & bit) != 0, (run & bit) != 0
        moved = jnp.where(
            row_set, pltpu.roll(cells, bit, 0), pltpu.roll(cells, count - bit, 0)
        )
        shift = bit * PATCH
        moved = jnp.where(
            run_set, pltpu.roll(moved, shift, 1), pltpu.roll(moved, LANES - shift, 1)
        )
        cells = jnp.where(row_set == run_set, cells, moved)
    return cells


def write_patches(tile, outs):
    bands = len(outs)
    species, planes = tile.counts
    for s in range(species):
        for p in range(planes):
            plane = swapped_tiles(tile(s, p))
            octets = PATCH // 8
            groups = plane.shape[0] // PATCH
            each = groups // bands
            for o in range(octets):
                col = ((s * planes + p) * octets + o) * LANES
                for index, out in enumerate(outs):
                    rows = [
                        plane[(g * octets + o) * 8 : (g * octets + o + 1) * 8]
                        for g in range(index * each, (index + 1) * each)
                    ]
                    out[:, col : col + LANES] = jnp.concatenate(rows, axis=0).astype(BF16)


class Tile:
    def __init__(self, read, counts):
        self.read, self.counts = read, counts

    def __call__(self, s, p):
        return self.read(s, p)


def packed_edges(order, cells, head_rows, tail_rows, width):
    species, planes, rows, _ = cells.shape
    tall = rows + 2 * width

    def body(ins, outs, _):
        middle, head, tail = ins
        lane = lax.broadcasted_iota(jnp.int32, (tall, LANES), 1)
        total = jnp.zeros((tall, LANES), F32)
        for s in range(species):
            for p in range(planes):
                plane = jnp.concatenate([head[s, p], middle[s, p], tail[s, p]], axis=0)
                slot = (s * planes + p) * width
                first = plane if slot == 0 else pltpu.roll(plane, slot, 1)
                last = pltpu.roll(plane, (LANES // 2 + slot + width) % LANES, 1)
                total = jnp.where((lane >= slot) & (lane < slot + width), first, total)
                start = LANES // 2 + slot
                total = jnp.where((lane >= start) & (lane < start + width), last, total)
        outs[0][...] = total

    return order.ride(body, [struct((tall, LANES), F32)], [cells, head_rows, tail_rows])


def stepped(order, cells, head_rows, tail_rows, from_left, from_right, width, halves):
    species, planes, rows, cols = cells.shape
    tall = rows + 2 * width
    patch_rows = rows // PATCH * (cols // PATCH) // halves
    features = species * planes * PATCH * PATCH

    def body(ins, outs, scratch):
        middle, head, tail, left, right = ins
        (final, *patches), (now, later) = outs, scratch
        lane = lax.broadcasted_iota(jnp.int32, (tall, LANES), 1)
        from_l, from_r = left[...], right[...]
        for s in range(species):
            for p in range(planes):
                slot = (s * planes + p) * width
                now[0, s, p] = jnp.concatenate([head[s, p], middle[s, p], tail[s, p]], axis=0)
                ahead = from_r if slot == 0 else pltpu.roll(from_r, LANES - slot, 1)
                behind = pltpu.roll(from_l, LANES // 2 - slot - width, 1)
                halo = jnp.where(lane < width, ahead, 0.0)
                now[1, s, p] = jnp.where(lane >= LANES - width, behind, halo)

        def neighbours(field, halo):
            up_f, down_f = pltpu.roll(field, 1, 0), pltpu.roll(field, tall - 1, 0)
            up_h, down_h = pltpu.roll(halo, 1, 0), pltpu.roll(halo, tall - 1, 0)
            before_f, before_h = pltpu.roll(field, 1, 1), pltpu.roll(halo, 1, 1)
            after_f, after_h = pltpu.roll(field, LANES - 1, 1), pltpu.roll(halo, LANES - 1, 1)
            first, last = lane == 0, lane == LANES - 1
            sum_f = up_f + down_f + jnp.where(first, before_h, before_f)
            sum_f = sum_f + jnp.where(last, after_h, after_f)
            sum_h = up_h + down_h + jnp.where(first, before_f, before_h)
            sum_h = sum_h + jnp.where(last, after_f, after_h)
            return sum_f, sum_h

        for step in range(STEPS):
            source, target = (now, later) if step % 2 == 0 else (later, now)

            def one_plane(p, carry):
                below, above = jnp.maximum(p - 1, 0), jnp.minimum(p + 1, planes - 1)
                beside = [neighbours(source[0, s, p], source[1, s, p]) for s in range(2)]
                for layer in range(2):
                    u, v = source[layer, 0, p], source[layer, 1, p]
                    lap = []
                    for s, centre in ((0, u), (1, v)):
                        total = source[layer, s, below] + source[layer, s, above]
                        lap.append(total + beside[s][layer] - 6.0 * centre)
                    growth = u * v * v
                    target[layer, 0, p] = u + TIME_STEP * (
                        SUBSTRATE_DIFFUSION * lap[0] - growth + FEED_RATE * (1.0 - u)
                    )
                    target[layer, 1, p] = v + TIME_STEP * (
                        CATALYST_DIFFUSION * lap[1] + growth - (FEED_RATE + KILL_RATE) * v
                    )
                return carry

            lax.fori_loop(0, planes, one_plane, 0)
        source = now if STEPS % 2 == 0 else later
        for s in range(species):
            for p in range(planes):
                final[s, p] = source[0, s, p, width : width + rows]
        write_patches(Tile(lambda s, p: final[s, p], (species, planes)), patches)

    return order.call(
        body,
        "stencil",
        [struct(cells.shape, F32)] + [struct((patch_rows, features), BF16)] * halves,
        [cells, head_rows, tail_rows, from_left, from_right],
        scratch=[pltpu.VMEM((2, species, planes, tall, LANES), F32)] * 2,
    )


def gelu_parts(preact):
    squared = preact * preact
    tangent = jnp.tanh(GELU_FACTOR * (preact + 0.044715 * preact * squared))
    return squared, tangent


def shards(state, embed, mlp, mom_embed, mom_mlp):
    dp_count, mp_count = lax.axis_size("dp"), lax.axis_size("mp")
    halves = 2 if dp_count % 2 == 0 else 1
    pairs = 2 if mp_count % 2 == 0 else 1
    wide = Digit("dp", dp_count // halves, halves)
    band = Digit("dp", 1, dp_count // halves)
    part = Digit("mp", pairs, mp_count // pairs)
    core = Digit("mp", 1, pairs)
    role = Digit("role", 1, lax.axis_size("role"))
    width = embed.shape[1] * dp_count
    own_rows, own_cols = embed.shape[1], embed.shape[2]
    half_width, part_cols = own_rows * band.size, own_cols * core.size
    to_solver, to_trainer = [(TRAINER, SOLVER)], [(SOLVER, TRAINER)]
    order = Order()

    def keep_arrived(arrived, own, index, following):
        def body(ins, outs, scratch):
            (sems,) = scratch
            solving = lax.axis_index("role") == SOLVER
            ahead = [
                pltpu.make_async_copy(ins[2].at[block], outs[1 + k], sems.at[1 + k])
                for k, block in enumerate(following)
            ]
            for copy in ahead:
                copy.start()

            @pl.when(solving)
            def _():
                outs[0][...] = ins[0][...]

            @pl.when(jnp.logical_not(solving))
            def _():
                mine = pltpu.make_async_copy(ins[1].at[index], outs[0], sems.at[0])
                mine.start()
                mine.wait()

            for copy in ahead:
                copy.wait()

        return order.call(
            body,
            "held",
            [struct(arrived.shape, BF16)] * (1 + len(following)),
            [arrived, own] + ([mlp] if following else []),
            left=(1, 2),
            scratch=[pltpu.SemaphoreType.DMA((1 + len(following),))],
        )

    def relayed(blocks):
        def body(ins, outs, _):
            for source, target in zip(ins, outs):
                target[...] = source[...]

        return order.ride(body, [struct(v.shape, v.dtype) for v in blocks], blocks)

    def own_pieces(block):
        return [block] + core.from_others(block), band.from_others(block)

    def merged(parts):
        return [jnp.concatenate(parts, axis=0)] if len(parts) > 1 else parts

    def held_matrix(own, relay):
        return Matrix([own] + [[rows] + core.from_others(rows) for rows in relay.results])

    cells = state[0]
    rows_in = cells.shape[2]
    features = cells.shape[0] * cells.shape[1] * PATCH * PATCH
    half_rows = rows_in // PATCH * (cells.shape[3] // PATCH) // 2

    def around(axis, step):
        count = lax.axis_size(axis)
        return [(i, (i + step) % count) for i in range(count)]

    def patches_of(ins, outs, _):
        counts = (cells.shape[0], cells.shape[1])
        write_patches(Tile(lambda s, p: ins[0][s, p], counts), outs[:2])
        outs[2][...] = ins[0][:, :, :STEPS]
        outs[3][...] = ins[0][:, :, rows_in - STEPS :]
        outs[4][...] = ins[0][...]

    def split_patches(own, arrived):
        def body(ins, outs, _):
            solving = lax.axis_index("role") == SOLVER
            position = lax.axis_index("mp")
            my_part, my_core = position // core.size, position % core.size
            for k in range(part.size):
                for t in range(core.size):
                    quarter = (my_part + k) % part.size * core.size
                    quarter = quarter + (my_core - t + core.size) % core.size
                    source = pl.ds(pl.multiple_of(quarter * own_cols, own_cols), own_cols)
                    cols = slice(t * own_cols, (t + 1) * own_cols)

                    @pl.when(solving)
                    def _():
                        outs[k][:, cols] = ins[0][:, source]

                    @pl.when(jnp.logical_not(solving))
                    def _():
                        outs[k][:, cols] = ins[1][:, source]

        return order.ride(
            body, [struct((half_rows, part_cols), BF16)] * part.size, [own, arrived]
        )

    def to_parts(cuts):
        return [cuts[0]] + [part.shifted(cuts[k], k) for k in range(1, part.size)]

    def slots(position, size, count):
        for k in range(size):
            slot = (position - k + size) % size
            yield k, pl.ds(pl.multiple_of(slot * count, count), count)

    def order_rows(pieces):
        def body(ins, outs, _):
            for k, rows in slots(lax.axis_index("mp") // core.size, part.size, half_rows):
                outs[0][rows, :] = ins[k][...]

        return order.ride(body, [struct((half_rows * part.size, part_cols), BF16)], pieces)

    def widened(rows):
        return [rows] + wide.from_others(rows)

    def pack(has_features, width_count):
        return struct((m, (own_cols if has_features else 0) + width_count * half_width), BF16)

    class Gather:
        def __init__(self, keep, sends, has_features, width_count):
            self.base = own_cols if has_features else 0
            self.width_count = width_count
            self.parts = [keep] + [core.shifted(sends[k - 1], k) for k in range(1, core.size)]

        def join(self):
            count = band.size if self.width_count else 1
            base = self.base

            def body(ins, outs, _):
                for c, ref in enumerate(ins):
                    rows = slice(c * m, (c + 1) * m)
                    for k in range(count):
                        if base:
                            outs[k][rows, :base] = ref[:, :base]
                        for index in range(self.width_count):
                            first = base + index * half_width + (-k) % band.size * own_rows
                            target = base + index * own_rows
                            outs[k][rows, target : target + own_rows] = ref[
                                :, first : first + own_rows
                            ]

            cols = base + self.width_count * own_rows
            self.joining = order.ride(
                body, [struct((m * core.size, cols), BF16)] * count, self.parts
            )

        def join_for_role(self):
            self.join()

            def body(ins, outs, _):
                for c, ref in enumerate(ins):
                    outs[0][c * m : (c + 1) * m, :] = ref[...]

            cols = self.base + self.width_count * half_width
            self.whole = order.ride(body, [struct((m * core.size, cols), BF16)], self.parts)

        def send_role_first(self):
            (whole,) = self.whole.results
            cuts = self.joining.results
            self.kept = cuts[0]
            self.banded = merged(
                [band.shifted(cuts[k % len(cuts)], k) for k in range(1, band.size)]
            )
            self.crossed = role.from_others(whole)

        def cut_crossed(self):
            base = self.base

            def body(ins, outs, _):
                for number, ref in enumerate(ins):
                    for k in range(band.size):
                        out = outs[number * band.size + k]
                        out[:, :base] = ref[:, :base]
                        for index in range(self.width_count):
                            first = base + index * half_width + (-k) % band.size * own_rows
                            target = base + index * own_rows
                            out[:, target : target + own_rows] = ref[:, first : first + own_rows]

            cols = base + self.width_count * own_rows
            self.cutting = order.ride(
                body,
                [struct((m * core.size, cols), BF16)] * (band.size * len(self.crossed)),
                self.crossed,
            )

        def band_crossed(self):
            self.arrived = []
            cuts = self.cutting.results
            for number in range(len(self.crossed)):
                own = cuts[number * band.size : (number + 1) * band.size]
                self.arrived += [own[0]] + merged(
                    [band.shifted(own[k], k) for k in range(1, band.size)]
                )

        def send(self):
            cuts = self.joining.results
            self.kept = cuts[0]
            self.banded = merged(
                [band.shifted(cuts[k % len(cuts)], k) for k in range(1, band.size)]
            )
            self.arrived = role.from_others(self.kept)

        def relay(self):
            self.relaying = relayed(self.banded)

        def forward(self, relayed_too=True):
            self.banded = self.relaying.results if relayed_too else self.banded
            for piece in self.banded:
                self.arrived = self.arrived + role.from_others(piece)

        def pieces(self):
            return [self.kept] + self.banded + self.arrived

    def product(lefts, left_col, rights, right_col):
        left = [ref[:, left_col : left_col + own_rows] for ref in lefts]
        right = [ref[:, right_col : right_col + own_cols] for ref in rights]
        return cols_dot(jnp.concatenate(left, axis=0), jnp.concatenate(right, axis=0))

    def begun_gradient(lefts, left_col, rights, right_col):
        count = len(lefts)

        def body(ins, outs, _):
            outs[0][...] = product(ins[:count], left_col, ins[count:], right_col)

        return order.ride(body, [struct((own_rows, own_cols), F32)], lefts + rights)

    def selected_state(own, arrived):
        def body(ins, outs, scratch):
            solving = lax.axis_index("role") == SOLVER
            (sem,) = scratch
            for chosen, source in ((solving, ins[0]), (jnp.logical_not(solving), ins[1])):

                @pl.when(chosen)
                def _():
                    copy = pltpu.make_async_copy(source, outs[0], sem)
                    copy.start()
                    copy.wait()

        scratch = [pltpu.SemaphoreType.DMA]
        outs = [struct(own.shape, F32)]
        return order.call(body, "state", outs, [own, arrived], in_hbm=(0,), scratch=scratch)[0]

    m = half_rows * part.size * wide.size
    total_rows = m * core.size * band.size * role.size
    loss_scale = float(total_rows) ** (-0.5)

    arrived_embed = lax.ppermute(embed[0], "role", to_solver)
    edge_struct = struct(cells.shape[:2] + (STEPS, cells.shape[3]), F32)
    *start_halves, first_rows, last_rows, cells = order.call(
        patches_of,
        "patches",
        [struct((half_rows, features), BF16)] * 2 + [edge_struct] * 2 + [struct(cells.shape, F32)],
        [cells],
    )
    arrived_start = lax.ppermute(start_halves[1], "role", to_trainer)
    head_rows = lax.ppermute(last_rows, "dp", around("dp", 1))
    tail_rows = lax.ppermute(first_rows, "dp", around("dp", -1))
    splitting = split_patches(start_halves[0], arrived_start)
    order.wait_for([head_rows, tail_rows])
    order.run("split")
    embed_kept, up_block, down_block = keep_arrived(arrived_embed, embed, 0, ((0, 0), (0, 1)))
    embed_own, embed_bands = own_pieces(embed_kept)
    arrived_up = lax.ppermute(up_block, "role", to_solver)
    arrived_down = lax.ppermute(down_block, "role", to_solver)
    ordering = order_rows(to_parts(splitting.results))
    edging = packed_edges(order, cells, head_rows, tail_rows, STEPS)
    order.run("order")
    input_parts = widened(*ordering.results)
    (edges,) = edging.results
    from_left = lax.ppermute(edges, "mp", around("mp", 1))
    from_right = lax.ppermute(edges, "mp", around("mp", -1))
    (up_kept,) = keep_arrived(arrived_up, mlp, (0, 0), ())
    up_own, up_bands = own_pieces(up_kept)
    relay = relayed(merged(embed_bands))
    order.wait_for([from_left, from_right] + input_parts[1:])
    order.run("relay")
    embed_held = held_matrix(embed_own, relay)
    final_cells, *end_halves = stepped(
        order, cells, head_rows, tail_rows, from_left, from_right, STEPS, 2
    )
    (down_kept,) = keep_arrived(arrived_down, mlp, (0, 1), ())
    down_own, down_bands = own_pieces(down_kept)
    up_relay = relayed(merged(up_bands))

    def embed_rows(ins, outs, _):
        parts, matrix = ins[: wide.size], ins[wide.size :]
        *inputs, mine, sent = outs
        position = lax.axis_index("dp") // band.size
        for k, rows in slots(position, wide.size, half_rows * part.size):
            for t in range(core.size):
                inputs[t][rows, :] = parts[k][:, t * own_cols : (t + 1) * own_cols]
        value = embed_held.to_width(matrix, jnp.concatenate([ref[...] for ref in inputs], axis=1))
        mine[...] = value
        sent[...] = value.astype(BF16)

    *inputs, embed_mine, embed_sum = order.call(
        embed_rows,
        "embed",
        [struct((m, own_cols), BF16)] * core.size
        + [struct((m, half_width), F32), struct((m, half_width), BF16)],
        input_parts + embed_held.flat,
    )
    embed_others = part.from_others(embed_sum)

    def core_slot(k):
        return slice((-k) % core.size * own_cols, ((-k) % core.size + 1) * own_cols)

    (arrived_end,) = role.from_others(end_halves[1])
    up_held = held_matrix(up_own, up_relay)
    copying = relayed([final_cells])

    def added(mine, refs, cols):
        total = mine[...]
        for ref in refs:
            total = total + ref[:, :cols].astype(F32)
        return total

    def up_rows(ins, outs, _):
        others, matrix = ins[1 : part.size], ins[part.size :]
        embedded, mine, sent = outs
        value = added(ins[0], others, half_width)
        embedded[...] = value
        hidden = up_held.to_cols(matrix, value.astype(BF16))
        mine[...] = hidden
        sent[...] = with_scalars(hidden, jnp.sum(value * value, axis=1, keepdims=True))

    embedded, up_mine, up_sum = order.call(
        up_rows,
        "up",
        [
            struct((m, half_width), F32),
            struct((m, part_cols), F32),
            struct((m, part_cols + LANES), BF16),
        ],
        [embed_mine] + embed_others + up_held.flat,
    )
    up_others = wide.from_others(up_sum)
    (arrived_cells,) = role.from_others(copying.results[0])
    order.wait_for(up_others + [arrived_cells])
    splitting = split_patches(end_halves[0], arrived_end)
    inputs_on = Gather(inputs[0], [inputs[(-k) % core.size] for k in range(1, core.size)], True, 0)
    inputs_on.join()
    relay = relayed(merged(down_bands))
    order.run("relay")
    down_held = held_matrix(down_own, relay)
    target_cuts = to_parts(splitting.results)
    inputs_on.send()

    def down_rows(ins, outs, _):
        value, others, matrix = ins[0][...], ins[2 : 1 + wide.size], ins[1 + wide.size :]
        hidden, mine, sent, scale, *packs = outs
        squares = jnp.sum(value * value, axis=1, keepdims=True)
        for ref in others:
            squares = squares + scalars_of(ref)
        recip = lax.rsqrt(squares / width + 1e-06)
        preact = added(ins[1], others, part_cols) * recip
        hidden[...] = preact
        normed = (value * recip).astype(BF16)
        _, tangent = gelu_parts(preact)
        active = (0.5 * preact * (1.0 + tangent)).astype(BF16)
        branch = down_held.to_width(matrix, active)
        mine[...] = branch
        sent[...] = branch.astype(BF16)
        scale[...] = jnp.broadcast_to(recip, scale.shape)
        for k in range(core.size):
            packs[k][:, :own_cols] = active[:, core_slot(k)]
            packs[k][:, own_cols:] = normed

    hidden_pre, down_mine, down_sum, scale, *active_packs = order.call(
        down_rows,
        "down",
        [
            struct((m, part_cols), F32),
            struct((m, half_width), F32),
            struct((m, half_width), BF16),
            struct((m, LANES), F32),
        ]
        + [pack(True, 1)] * core.size,
        [embedded, up_mine] + up_others + down_held.flat,
    )
    down_others = part.from_others(down_sum)
    active_on = Gather(active_packs[0], active_packs[1:], True, 1)
    active_on.join()
    inputs_on.relay()
    order.wait_for(inputs_on.arrived)

    def predict_rows(ins, outs, _):
        aims, ins = ins[: part.size], ins[part.size :]
        others, matrix = ins[2 : 1 + part.size], ins[1 + part.size :]
        mine, sent, stream = outs
        value = (ins[0][...] + added(ins[1], others, half_width)).astype(BF16)
        stream[...] = value
        mine[...] = embed_held.to_cols(matrix, value)
        position = lax.axis_index("dp") // band.size * part.size
        for k, ref in enumerate(aims):
            slot = (lax.axis_index("mp") // core.size - k + part.size) % part.size
            rows = pl.ds(pl.multiple_of((position + slot) * half_rows, half_rows), half_rows)
            mine[rows, :] = mine[rows, :] - ref[...].astype(F32)
        sent[...] = mine[...].astype(BF16)

    predict_mine, predict_sum, stream = order.call(
        predict_rows,
        "predict",
        [
            struct((m, part_cols), F32),
            struct((m, part_cols), BF16),
            struct((m, half_width), BF16),
        ],
        target_cuts + [embedded, down_mine] + down_others + embed_held.flat,
    )
    predict_others = wide.from_others(predict_sum)
    inputs_on.forward()
    active_on.send()
    active_on.relay()
    order.wait_for(active_on.arrived)

    def residual_rows(ins, outs, _):
        inputs, ins = ins[: core.size], ins[core.size :]
        mine_in, others, ins = ins[0], ins[1 : wide.size], ins[wide.size :]
        stream, matrix = ins[0], ins[1:]
        mine, sent, *packs = outs
        known = jnp.concatenate([ref[...] for ref in inputs], axis=1).astype(F32)
        value = ((known + added(mine_in, others, part_cols)) * loss_scale).astype(BF16)
        for k in range(core.size):
            packs[k][:, :own_cols] = value[:, core_slot(k)]
            packs[k][:, own_cols:] = stream[...]
        grad = embed_held.to_width(matrix, value)
        mine[...] = grad
        sent[...] = grad.astype(BF16)

    stream_mine, stream_sum, *residual_packs = order.call(
        residual_rows,
        "residual",
        [struct((m, half_width), F32), struct((m, half_width), BF16)]
        + [pack(True, 1)] * core.size,
        inputs + [predict_mine] + predict_others + [stream] + embed_held.flat,
    )
    stream_others = part.from_others(stream_sum)

    active_on.forward()
    residual_on = Gather(residual_packs[0], residual_packs[1:], True, 1)
    residual_on.join_for_role()
    order.wait_for(inputs_on.arrived)

    def hidden_rows(ins, outs, _):
        others, matrix = ins[1 : part.size], ins[part.size :]
        grad, mine, sent, rounded_out = outs
        value = added(ins[0], others, half_width)
        grad[...] = value
        rounded = value.astype(BF16)
        back = down_held.to_cols(matrix, rounded)
        mine[...] = back
        sent[...] = back.astype(BF16)
        rounded_out[...] = rounded

    stream_grad, back_mine, back_sum, stream_sent = order.call(
        hidden_rows,
        "hidden",
        [
            struct((m, half_width), F32),
            struct((m, part_cols), F32),
            struct((m, part_cols), BF16),
            struct((m, half_width), BF16),
        ],
        [stream_mine] + stream_others + down_held.flat,
    )
    back_others = wide.from_others(back_sum)
    residual_on.send_role_first()
    order.wait_for(active_on.arrived + residual_on.banded + residual_on.crossed)

    def normed_rows(ins, outs, _):
        stream_sent, others, matrix = ins[2], ins[3 : 2 + wide.size], ins[2 + wide.size :]
        mine, inner, sent, *packs = outs
        preact = ins[0][...]
        squared, tangent = gelu_parts(preact)
        slope = 0.5 * (1.0 + tangent) + 0.5 * preact * (1.0 - tangent * tangent) * GELU_FACTOR * (
            1.0 + 3.0 * 0.044715 * squared
        )
        value = (added(ins[1], others, part_cols) * slope).astype(BF16)
        for k in range(core.size):
            packs[k][:, :own_cols] = value[:, core_slot(k)]
            packs[k][:, own_cols:] = stream_sent[...]
        grad = up_held.to_width(matrix, value)
        mine[...] = grad
        both = jnp.sum(value.astype(F32) * preact, axis=1, keepdims=True)
        inner[...] = jnp.broadcast_to(both, inner.shape)
        sent[...] = with_scalars(grad, both)

    normed_mine, inner_mine, normed_sum, *hidden_packs = order.call(
        normed_rows,
        "normed",
        [
            struct((m, half_width), F32),
            struct((m, LANES), F32),
            struct((m, half_width + LANES), BF16),
        ]
        + [pack(True, 1)] * core.size,
        [hidden_pre, back_mine, stream_sent] + back_others + up_held.flat,
    )
    normed_others = part.from_others(normed_sum)
    hidden_on = Gather(hidden_packs[0], hidden_packs[1:], True, 1)
    hidden_on.join()
    order.run("join")
    hidden_on.send()
    hidden_kept_arrived = list(hidden_on.arrived)
    hidden_on.forward(False)
    residual_on.cut_crossed()

    def embed_grad_rows(ins, outs, _):
        value, grad, scale_ref, mine, inner_ref, *others = ins
        normed_grad = added(mine, others, half_width)
        inner = inner_ref[:, :1]
        for ref in others:
            inner = inner + scalars_of(ref)
        recip = scale_ref[:, :1]
        outs[0][...] = (
            grad[...] + recip * normed_grad - value[...] * (recip * recip) * (inner / width)
        ).astype(BF16)

    (embed_sent,) = order.call(
        embed_grad_rows,
        "embed_grad",
        [pack(False, 1)],
        [embedded, stream_grad, scale, normed_mine, inner_mine] + normed_others,
    )
    embed_sent_on = Gather(embed_sent, [embed_sent] * (core.size - 1), False, 1)
    embed_sent_on.join()
    order.wait_for(hidden_kept_arrived)
    order.run("join")
    embed_sent_on.send()
    embed_sent_on.forward(False)
    residual_on.band_crossed()
    all_residual = residual_on.pieces()
    embed_term = begun_gradient(all_residual, own_cols, all_residual, 0)
    state_out = selected_state(final_cells, arrived_cells)

    def updated(name, products, momentum, weight, term=()):
        arrays = [v for _, lefts, _, rights, _ in products for v in lefts + rights] + list(term)
        cuts = 2
        step = own_rows // cuts
        blocks = len(products)

        def body(ins, outs, scratch):
            mom_new, weight_new, sems = scratch
            mom, old = ins[len(arrays)], ins[len(arrays) + 1]
            copies, first = [], 0
            for block, (index, lefts, left_col, rights, right_col) in enumerate(products):
                middle, last = first + len(lefts), first + len(lefts) + len(rights)
                total = product(ins[first:middle], left_col, ins[middle:last], right_col)
                first = last
                for ref in ins[first : first + len(term)]:
                    total = total + ref[...]
                for cut in range(cuts):
                    rows = slice(cut * step, (cut + 1) * step)
                    fresh = MOMENTUM_DECAY * mom[index][rows] + total[rows]
                    mom_new[block, rows, :] = fresh
                    weight_new[block, rows, :] = (
                        old[index][rows].astype(F32) - LEARNING_RATE * fresh
                    ).astype(BF16)
                    for number, source in enumerate((mom_new, weight_new)):
                        copies.append(
                            pltpu.make_async_copy(
                                source.at[block, pl.ds(cut * step, step)],
                                outs[number].at[index].at[pl.ds(cut * step, step)],
                                sems.at[(block * cuts + cut) * 2 + number],
                            )
                        )
                        copies[-1].start()
            for copy in copies:
                copy.wait()

        return order.call(
            body,
            name,
            [struct(momentum.shape, F32), struct(weight.shape, BF16)],
            arrays + [momentum, weight],
            in_hbm=(0, 1),
            scratch=[
                pltpu.VMEM((blocks, own_rows, own_cols), F32),
                pltpu.VMEM((blocks, own_rows, own_cols), BF16),
                pltpu.SemaphoreType.DMA((2 * cuts * blocks,)),
            ],
        )

    all_inputs, all_active = inputs_on.pieces(), active_on.pieces()
    all_hidden, all_embed_sent = hidden_on.pieces(), embed_sent_on.pieces()
    mom_mlp_out, mlp_out = updated(
        "update_mlp",
        [
            ((0, 0), all_active, own_cols, all_hidden, 0),
            ((0, 1), all_hidden, own_cols, all_active, 0),
        ],
        mom_mlp,
        mlp,
    )
    mom_embed_out, embed_out = updated(
        "update_embed",
        [(0, all_embed_sent, 0, all_inputs, 0)],
        mom_embed,
        embed,
        embed_term.results,
    )
    return (state_out, embed_out, mlp_out, mom_embed_out, mom_mlp_out)


def solution(mesh):
    placed = (
        P("role", None, None, "dp", "mp"),
        P("role", "dp", "mp"),
        P("role", None, "dp", "mp"),
        P("role", "dp", "mp"),
        P("role", None, "dp", "mp"),
    )
    return jax.shard_map(
        shards,
        mesh=mesh,
        in_specs=placed,
        out_specs=(
            P(None, None, "dp", "mp"),
            P("role", "dp", "mp"),
            P("role", None, "dp", "mp"),
            P("role", "dp", "mp"),
            P("role", None, "dp", "mp"),
        ),
        check_vma=False,
    )
```
